256 devices in a mesh: dp: 16 (over x, y), fsdp: 16 (over z, core).
Axes of the slice: x: 4, y: 4, z: 8, core: 2. Of those that a mesh axis runs over, the one named last changes fastest.
Arguments:
- tokens: bfloat16 [65536, 5120], P(('dp', 'fsdp')), may hold values from -6 to 6
- cotangent: bfloat16 [65536, 1024], P(('dp', 'fsdp')), may hold values from -6 to 6
- block_adapter: int32 [512, 1], P(('dp', 'fsdp')), may hold values from 0 to 63
- live_length: int32 [512], P(('dp', 'fsdp')), may hold values from 1 to 128, as said below
- storage_row_of_adapter: int32 [64], replicated, may hold values from 0 to 63, each once
- value_weight: bfloat16 [5120, 1024], P('fsdp'), may hold values from -0.1875 to 0.1875
- adapter_down_weight: bfloat16 [64, 5120, 64], P('dp', 'fsdp'), may hold values from -0.078125 to 0.078125
- adapter_up_weight: bfloat16 [64, 64, 1024], P('dp', None, 'fsdp'), may hold values from -0.75 to 0.75
Outputs:
- input_grad: bfloat16 [65536, 5120], P(('dp', 'fsdp'))
- grad_down: float32 [64, 5120, 64], P('dp', 'fsdp')
- grad_up: float32 [64, 64, 1024], P('dp', None, 'fsdp')
The draws below stay inside these ranges and needn't reach their ends.
Inputs may be any that keep to these rules, and one draw needn't show every extreme that they name: `block_adapter`: every adapter is named by some block. A permutation; adapter e is stored at row storage_row_of_adapter[e]. `live_length`: some block is full and some block has one live position.
All inputs are finite; a program needn't handle non-finite values.
Results may differ from the reference program's by a relative error of at most 0.0048.
Values may be sent and summed in bfloat16 or wider, within the bound.
No kernel may reach another device: no remote copies, remote signals or barrier semaphores. Data moves between devices by JAX's collectives and lax.ppermute only.
A program may use at most 128 MiB of HBM per device.

```python
import jax
import jax.numpy as jnp
from jax import lax

MODEL_WIDTH = 5120
VALUE_WIDTH = 1024
ADAPTER_RANK = 64
ADAPTER_TOTAL = 64
BLOCK_LENGTH = 128
TOKENS = 65536
NBLK = 512


def draw_live_length(key, part):
    lengths = jax.random.randint(key, (NBLK,), 1, BLOCK_LENGTH + 1)
    lengths = lengths.at[0].set(BLOCK_LENGTH)
    lengths = lengths.at[1].set(1)
    return lengths.astype(jnp.int32)


def block_levels(rng, shape, cuts, low, high):
    gain, own = 1.0, jax.random.fold_in(rng, 6)
    for position, shards_of in cuts:
        steps = jnp.exp(jax.random.uniform(jax.random.fold_in(own, position), (shards_of,), jnp.float32, low / len(cuts), high / len(cuts)))
        gain = gain * jnp.repeat(steps, shape[position] // shards_of).reshape([-1 if axis == position else 1 for axis in range(len(shape))])
    return gain


def distinct(own_key, rows, amount, top, lift):
    order = jax.random.permutation(jax.random.fold_in(own_key, 1), amount)
    favour = order
    for power in range(3):
        favour = favour * favour // amount
    favour = favour * lift // amount
    chance = jax.random.randint(jax.random.fold_in(own_key, 2), (rows, amount), 0, 4096) + favour
    holders = jax.random.permutation(jax.random.fold_in(own_key, 3), rows)[jnp.arange(amount) % rows]
    chance = jnp.where(jnp.arange(rows)[:, None] == holders[None, :], 1 << 14, chance)
    merit = chance * amount + jnp.arange(amount)
    return lax.top_k(merit.astype(jnp.int32), top)[1].astype(jnp.int32)


def bell_draw(stream_key, shape, spread, bound, shards=(), kind=jnp.bfloat16):
    values = jax.random.normal(stream_key, shape, jnp.float32) * spread
    if len(shards) > 0:
        values = block_levels(stream_key, shape, shards, -0.22, 0.18) * values
    return jnp.clip(values, min=-bound, max=bound).astype(kind)


def setup_inputs(seed: int = 0) -> dict:
    streams_of = jax.random.split(jax.random.key(seed), 9)
    return {
        "tokens": bell_draw(streams_of[0], (TOKENS, MODEL_WIDTH), 1.0, 6.0, ((0, 256),)),
        "cotangent": bell_draw(streams_of[1], (TOKENS, VALUE_WIDTH), 1.0, 6.0, ((0, 256),)),
        "block_adapter": distinct(streams_of[2], NBLK, ADAPTER_TOTAL, 1, 256),
        "live_length": draw_live_length(jax.random.fold_in(streams_of[8], 71), 0),
        "storage_row_of_adapter": jax.random.permutation(streams_of[4], ADAPTER_TOTAL).astype(jnp.int32),
        "value_weight": bell_draw(streams_of[5], (MODEL_WIDTH, VALUE_WIDTH), VALUE_WIDTH ** -0.5, 0.1875, ((0, 16),)),
        "adapter_down_weight": bell_draw(streams_of[6], (ADAPTER_TOTAL, MODEL_WIDTH, ADAPTER_RANK), MODEL_WIDTH ** -0.5, 0.078125, ((0, 16), (1, 16))),
        "adapter_up_weight": bell_draw(streams_of[7], (ADAPTER_TOTAL, ADAPTER_RANK, VALUE_WIDTH), ADAPTER_RANK ** -0.5, 0.75, ((0, 16), (2, 16))),
    }


adapter_scale = 2.0


def reference(tokens, cotangent, block_adapter, live_length, storage_row_of_adapter, value_weight, adapter_down_weight, adapter_up_weight):
    block_count = tokens.shape[0] // BLOCK_LENGTH
    token_blocks = tokens.reshape(block_count, BLOCK_LENGTH, MODEL_WIDTH)
    grad_blocks = cotangent.reshape(block_count, BLOCK_LENGTH, VALUE_WIDTH)
    live_mask = jnp.arange(BLOCK_LENGTH, dtype=jnp.int32)[None, :] < live_length[:, None]
    block_slots = storage_row_of_adapter[block_adapter[:, 0]].astype(jnp.int32)

    def step(carry, item):
        grad_down, grad_up = carry
        token_rows, grad_rows, live_rows, storage_index = item
        masked_rows = jnp.where(live_rows[:, None], grad_rows, jnp.zeros_like(grad_rows))
        down_matrix = adapter_down_weight[storage_index]
        up_matrix = adapter_up_weight[storage_index]
        down_hidden = jnp.dot(token_rows, down_matrix, preferred_element_type=jnp.float32).astype(jnp.bfloat16)
        backward_hidden = (adapter_scale * jnp.dot(masked_rows, up_matrix.T, preferred_element_type=jnp.float32)).astype(jnp.bfloat16)
        adapter_input_gradient = jnp.dot(backward_hidden, down_matrix.T, preferred_element_type=jnp.float32).astype(jnp.bfloat16)
        adapter_input_gradient = lax.optimization_barrier(adapter_input_gradient)
        frozen_gradient = jnp.dot(masked_rows, value_weight.T, preferred_element_type=jnp.float32)
        input_matrix = (frozen_gradient + adapter_input_gradient.astype(jnp.float32)).astype(jnp.bfloat16)
        down_term = jnp.dot(token_rows.T, backward_hidden, preferred_element_type=jnp.float32) / BLOCK_LENGTH
        up_product = jnp.dot(down_hidden.T, masked_rows, preferred_element_type=jnp.float32) * (adapter_scale / BLOCK_LENGTH)
        grad_down = grad_down.at[storage_index].add(down_term)
        grad_up = grad_up.at[storage_index].add(up_product)
        return (grad_down, grad_up), input_matrix

    start = (jnp.zeros((ADAPTER_TOTAL, MODEL_WIDTH, ADAPTER_RANK), jnp.float32), jnp.zeros((ADAPTER_TOTAL, ADAPTER_RANK, VALUE_WIDTH), jnp.float32))
    (grad_down, grad_up), input_blocks = lax.scan(step, start, (token_blocks, grad_blocks, live_mask, block_slots))
    input_grad = input_blocks.reshape(block_count * BLOCK_LENGTH, MODEL_WIDTH)
    return input_grad, grad_down, grad_up
```

```python
import jax
import jax.numpy as jnp
from jax import lax
from jax.experimental import pallas as pl
from jax.experimental.pallas import tpu as pltpu
from jax.sharding import Mesh
from jax.sharding import PartitionSpec as P

BLOCK_LENGTH = 128
adapter_scale = 2.0

EVERY = ("x", "y", "u", "v", "c")
DP = ("x", "y")
FSDP = ("u", "v", "c")
SPREAD = ("u", "x", "y")
CELL = ("v", "c", "x", "y")
GROUP = 384
BIG = pltpu.CompilerParams(vmem_limit_bytes=40 * 1024 * 1024)


def select_kernel(target_ref, table_ref, out_ref):
    rows = out_ref.shape[0]
    entries = table_ref.shape[1]
    lane = lax.broadcasted_iota(jnp.int32, (rows, entries), 1)
    pick = jnp.where(lane == target_ref[...], 1.0, 0.0).astype(jnp.bfloat16)
    for u in range(table_ref.shape[0]):
        part = jnp.dot(pick, table_ref[u], preferred_element_type=jnp.float32)
        out_ref[:, u * GROUP : (u + 1) * GROUP] = part.astype(jnp.bfloat16)


def collect_kernel(target_ref, terms_ref, out_ref):
    entries = out_ref.shape[1]
    rows = terms_ref.shape[0]
    sub = lax.broadcasted_iota(jnp.int32, (entries, rows), 0)
    pick = jnp.where(sub == target_ref[...], 1.0, 0.0).astype(jnp.bfloat16)
    for u in range(out_ref.shape[0]):
        part = jnp.dot(
            pick, terms_ref[:, u * GROUP : (u + 1) * GROUP], preferred_element_type=jnp.float32
        )
        out_ref[u] = part.astype(jnp.bfloat16)


def finish_kernel(parts_ref, down_ref, up_ref):
    for d in range(16):
        total = parts_ref[0, d].astype(jnp.float32)
        for u in range(1, 4):
            total = total + parts_ref[u, d].astype(jnp.float32)
        for s in range(4):
            rows = total[4 * s : 4 * s + 4]
            down_ref[s, 4 * d : 4 * d + 4, :] = rows[:, :320]
            up_ref[s, 4 * d : 4 * d + 4, :] = rows[:, 320:]


def masked_rows(live_ref, cotangent_ref):
    count = cotangent_ref.shape[0]
    row = lax.broadcasted_iota(jnp.int32, (count, 1), 0)
    limit = jnp.where(row < BLOCK_LENGTH, live_ref[0], live_ref[1] + BLOCK_LENGTH)
    grads = cotangent_ref[...]
    return jnp.where(row < limit, grads, jnp.zeros_like(grads))


def block_kernel(live_ref, tokens_ref, cotangent_ref, maps_ref, terms_ref, back_ref, wide_ref, grads):
    grads[...] = masked_rows(live_ref, cotangent_ref)
    lane = lax.broadcasted_iota(jnp.int32, (128, 128), 1)
    low = lane < 64
    contract = (((1,), (1,)), ((), ()))
    down = jnp.zeros((256, 128), jnp.float32)
    back = jnp.zeros((256, 128), jnp.float32)
    for j in range(8):
        u, v = j // 2, j % 2
        tiles = [
            maps_ref[2 * v + c, :, u * GROUP + 128 * k : u * GROUP + 128 * k + 128].astype(jnp.float32)
            for c in range(2)
            for k in range(3)
        ]
        turned = [None, None] + [pltpu.roll(t, 64, 1) for t in tiles[2:]]
        wide = [
            tiles[0],
            tiles[1],
            jnp.where(low, tiles[2], turned[3]),
            jnp.where(low, turned[3], turned[4]),
            jnp.where(low, turned[4], turned[5]),
        ]
        up = jnp.where(low, turned[2], tiles[5]).astype(jnp.bfloat16)
        for k in range(5):
            wide_ref[j, :, 128 * k : 128 * k + 128] = wide[k].astype(jnp.bfloat16)
        down = down + lax.dot_general(
            tokens_ref[:, 640 * j : 640 * j + 640],
            wide_ref[j],
            contract,
            preferred_element_type=jnp.float32,
        )
        back = back + lax.dot_general(
            grads[:, 128 * j : 128 * j + 128], up, contract, preferred_element_type=jnp.float32
        )
    row = lax.broadcasted_iota(jnp.int32, (256, 128), 0)
    column = lax.broadcasted_iota(jnp.int32, (256, 128), 1)
    own = (row // 128) == ((column // 4) % 2)
    down = jnp.where(own, down, 0.0).astype(jnp.bfloat16)
    back = jnp.where(own, adapter_scale * back, 0.0).astype(jnp.bfloat16)
    back_ref[...] = back
    over_rows = (((0,), (0,)), ((), ()))
    for j in range(8):
        u, v = j // 2, j % 2
        part = lax.dot_general(
            back,
            tokens_ref[:, 640 * j : 640 * j + 640],
            over_rows,
            preferred_element_type=jnp.float32,
        ) * (1.0 / BLOCK_LENGTH)
        up = lax.dot_general(
            down, grads[:, 128 * j : 128 * j + 128], over_rows, preferred_element_type=jnp.float32
        ) * (adapter_scale / BLOCK_LENGTH)
        piece = [part[:, 128 * k : 128 * k + 128] for k in range(5)]
        turned = [None, None] + [pltpu.roll(t, 64, 1) for t in piece[2:]]
        up_turned = pltpu.roll(up, 64, 1)
        out = [
            piece[0],
            piece[1],
            jnp.where(low, piece[2], up_turned),
            jnp.where(low, turned[2], turned[3]),
            jnp.where(low, turned[3], turned[4]),
            jnp.where(low, turned[4], up),
        ]
        for c in range(2):
            for k in range(3):
                at = u * GROUP + 128 * k
                terms_ref[2 * v + c, :, at : at + 128] = out[3 * c + k].astype(jnp.bfloat16)


def input_kernel(live_ref, cotangent_ref, back_ref, wide_ref, weight_ref, out_ref, grads):
    @pl.when(pl.program_id(0) == 0)
    def _():
        grads[...] = masked_rows(live_ref, cotangent_ref)

    low_rank = jnp.dot(back_ref[...], wide_ref[0], preferred_element_type=jnp.float32)
    low_rank = low_rank.astype(jnp.bfloat16).astype(jnp.float32)
    weight = weight_ref[...].reshape(640, 1024)
    frozen = lax.dot_general(
        grads[...], weight, (((1,), (1,)), ((), ())), preferred_element_type=jnp.float32
    )
    out_ref[...] = (frozen + low_rank).astype(jnp.bfloat16)


def on_device(
    tokens,
    cotangent,
    block_adapter,
    live_length,
    storage_row_of_adapter,
    value_weight,
    adapter_down_weight,
    adapter_up_weight,
):
    bf16, f32 = jnp.bfloat16, jnp.float32
    named = block_adapter[:, :1] == jnp.arange(64, dtype=jnp.int32)[None, :]
    block_slots = jnp.sum(jnp.where(named, storage_row_of_adapter[None, :], 0), axis=1)
    slot_tile = jnp.broadcast_to(jnp.pad(block_slots, (0, 126))[None, :], (8, 128))
    cell_slots = lax.all_gather(slot_tile, CELL, axis=0, tiled=False)[:, 0, :2]
    target = (cell_slots.reshape(128, 1) * 4 + jnp.arange(4, dtype=jnp.int32)[None, :]).reshape(512)

    own = jnp.concatenate(
        [jnp.transpose(adapter_down_weight, (0, 2, 1)), adapter_up_weight], axis=2
    )
    own = jnp.transpose(own.reshape(4, 16, 4, GROUP), (1, 0, 2, 3)).reshape(1, 16, 16, GROUP)
    own = jnp.broadcast_to(own, (4, 16, 16, GROUP)).reshape(64, 16, GROUP)
    table = lax.all_to_all(own, SPREAD, split_axis=0, concat_axis=0, tiled=True)
    table = table.reshape(4, 256, GROUP)

    chosen = pl.pallas_call(
        select_kernel,
        out_shape=jax.ShapeDtypeStruct((512, 4 * GROUP), bf16),
        compiler_params=BIG,
        name="select_rows",
    )(target.reshape(512, 1), table)
    maps = lax.all_to_all(
        chosen.reshape(64, 8, 4 * GROUP), CELL, split_axis=0, concat_axis=0, tiled=True
    ).reshape(4, 128, 4 * GROUP)

    smem = pl.BlockSpec(memory_space=pltpu.SMEM)
    vmem = pl.BlockSpec(memory_space=pltpu.VMEM)
    terms, back, wide = pl.pallas_call(
        block_kernel,
        out_shape=(
            jax.ShapeDtypeStruct((4, 128, 4 * GROUP), bf16),
            jax.ShapeDtypeStruct((256, 128), bf16),
            jax.ShapeDtypeStruct((8, 128, 640), bf16),
        ),
        in_specs=[smem, vmem, vmem, vmem],
        scratch_shapes=[pltpu.VMEM((256, 1024), bf16)],
        compiler_params=BIG,
        cost_estimate=pl.CostEstimate(flops=10**9, bytes_accessed=9 * 10**6, transcendentals=0),
        name="block_terms",
    )(live_length, tokens, cotangent, maps)

    returned = lax.all_to_all(
        terms.reshape(64, 8, 4 * GROUP), CELL, split_axis=0, concat_axis=0, tiled=True
    ).reshape(512, 4 * GROUP)
    sums = pl.pallas_call(
        collect_kernel,
        out_shape=jax.ShapeDtypeStruct((4, 256, GROUP), bf16),
        compiler_params=BIG,
        name="collect_rows",
    )(target.reshape(1, 512), returned)
    parts = lax.all_to_all(
        sums.reshape(64, 16, GROUP), SPREAD, split_axis=0, concat_axis=0, tiled=True
    ).reshape(4, 16, 16, GROUP)
    down, grad_up = pl.pallas_call(
        finish_kernel,
        out_shape=(
            jax.ShapeDtypeStruct((4, 64, 320), f32),
            jax.ShapeDtypeStruct((4, 64, 64), f32),
        ),
        compiler_params=BIG,
        name="finish_sums",
    )(parts)
    grad_down = jnp.transpose(down, (0, 2, 1))

    half = lax.all_gather(value_weight, ("u", "v"), axis=0, tiled=False)
    weight = lax.all_gather(half, "c", axis=0, tiled=False)
    input_grad = pl.pallas_call(
        input_kernel,
        grid=(8,),
        out_shape=jax.ShapeDtypeStruct((256, 5120), bf16),
        in_specs=[
            smem,
            pl.BlockSpec((256, 1024), lambda j: (0, 0)),
            pl.BlockSpec((256, 128), lambda j: (0, 0)),
            pl.BlockSpec((1, 128, 640), lambda j: (j, 0, 0)),
            pl.BlockSpec((2, 1, 320, 1024), lambda j: (0, j, 0, 0)),
        ],
        out_specs=pl.BlockSpec((256, 640), lambda j: (0, j)),
        scratch_shapes=[pltpu.VMEM((256, 1024), bf16)],
        compiler_params=BIG,
        cost_estimate=pl.CostEstimate(
            flops=3 * 10**9, bytes_accessed=16 * 10**6, transcendentals=0
        ),
        name="input_grad",
    )(live_length, cotangent, back, wide, weight)
    return (input_grad, grad_down, grad_up)


def solution(mesh):
    fine = Mesh(mesh.devices.reshape(4, 4, 4, 2, 2), EVERY)
    placed = (
        P(EVERY, None),
        P(EVERY, None),
        P(EVERY, None),
        P(EVERY),
        P(),
        P(FSDP, None),
        P(DP, FSDP, None),
        P(DP, None, FSDP),
    )
    return jax.shard_map(
        on_device,
        mesh=fine,
        in_specs=placed,
        out_specs=(P(EVERY, None), P(DP, FSDP, None), P(DP, None, FSDP)),
        check_vma=False,
    )
```

```python
import jax
import jax.numpy as jnp
from jax import lax
from jax.experimental import pallas as pl
from jax.experimental.pallas import tpu as pltpu
from jax.sharding import Mesh
from jax.sharding import PartitionSpec as P

BLOCK_LENGTH = 128
adapter_scale = 2.0

EVERY = ("x", "y", "u", "v", "c")
DP = ("x", "y")
COLUMN = ("u", "v")
FSDP = ("u", "v", "c")
CELL = ("v", "c", "x", "y")
HEAR = [[((z - k) % 8 if z % 2 == 0 else (z + k) % 8, z) for z in range(8)] for k in range(4)]
TELL = [[(b, a) for a, b in pairs] for pairs in HEAR]
GROUP = 384
BIG = pltpu.CompilerParams(vmem_limit_bytes=40 * 1024 * 1024)


def select_kernel(target_ref, table0, table1, table2, table3, out_ref):
    rows = out_ref.shape[0]
    lane = lax.broadcasted_iota(jnp.int32, (rows, 256), 1)
    pick = jnp.where(lane == target_ref[...], 1.0, 0.0).astype(jnp.bfloat16)
    for k, table in enumerate((table0, table1, table2, table3)):
        part = jnp.dot(pick, table[...], preferred_element_type=jnp.float32)
        out_ref[:, k * GROUP : (k + 1) * GROUP] = part.astype(jnp.bfloat16)


def collect_kernel(target_ref, terms_ref, out0, out1, out2, out3):
    rows = terms_ref.shape[0]
    sub = lax.broadcasted_iota(jnp.int32, (256, rows), 0)
    pick = jnp.where(sub == target_ref[...], 1.0, 0.0).astype(jnp.bfloat16)
    for k, out in enumerate((out0, out1, out2, out3)):
        part = jnp.dot(
            pick, terms_ref[:, k * GROUP : (k + 1) * GROUP], preferred_element_type=jnp.float32
        )
        out[...] = part.astype(out.dtype)


def merge_kernel(part0, part1, part2, part3, out_ref):
    f32 = jnp.float32
    out_ref[...] = (part0[...] + part1[...].astype(f32)) + (
        part2[...].astype(f32) + part3[...].astype(f32)
    )


def finish_kernel(parts_ref, down_ref, up_ref):
    for d in range(16):
        for s in range(4):
            rows = parts_ref[d, 4 * s : 4 * s + 4, :]
            down_ref[s, 4 * d : 4 * d + 4, :] = rows[:, :320]
            up_ref[s, 4 * d : 4 * d + 4, :] = rows[:, 320:]


def masked_rows(live_ref, cotangent_ref):
    count = cotangent_ref.shape[0]
    row = lax.broadcasted_iota(jnp.int32, (count, 1), 0)
    limit = jnp.where(row < BLOCK_LENGTH, live_ref[0], live_ref[1] + BLOCK_LENGTH)
    grads = cotangent_ref[...]
    return jnp.where(row < limit, grads, jnp.zeros_like(grads))


def shard_of(cell, j):
    z = cell * 2 + (8 - j if j < 4 else 1 + j - 4)
    return lax.rem(z, 8)


def block_kernel(
    cell_ref, live_ref, tokens_ref, cotangent_ref, maps_ref, terms_ref, back_ref, wide_ref, grads
):
    grads[...] = masked_rows(live_ref, cotangent_ref)
    shards = [shard_of(cell_ref[0], j) for j in range(8)]

    def token_columns(j):
        return tokens_ref[:, pl.ds(pl.multiple_of(shards[j] * 640, 128), 640)]

    def grad_columns(j):
        return grads[:, pl.ds(pl.multiple_of(shards[j] * 128, 128), 128)]

    lane = lax.broadcasted_iota(jnp.int32, (128, 128), 1)
    low = lane < 64
    contract = (((1,), (1,)), ((), ()))
    down = jnp.zeros((256, 128), jnp.float32)
    back = jnp.zeros((256, 128), jnp.float32)
    for j in range(8):
        u, v = j % 4, j // 4
        tiles = [
            maps_ref[2 * v + c, :, u * GROUP + 128 * k : u * GROUP + 128 * k + 128].astype(jnp.float32)
            for c in range(2)
            for k in range(3)
        ]
        turned = [None, None] + [pltpu.roll(t, 64, 1) for t in tiles[2:]]
        wide = [
            tiles[0],
            tiles[1],
            jnp.where(low, tiles[2], turned[3]),
            jnp.where(low, turned[3], turned[4]),
            jnp.where(low, turned[4], turned[5]),
        ]
        up = jnp.where(low, turned[2], tiles[5]).astype(jnp.bfloat16)
        wide = jnp.concatenate(wide, axis=1).astype(jnp.bfloat16)
        wide_ref[shards[j]] = wide
        down = down + lax.dot_general(
            token_columns(j),
            wide,
            contract,
            preferred_element_type=jnp.float32,
        )
        back = back + lax.dot_general(
            grad_columns(j), up, contract, preferred_element_type=jnp.float32
        )
    row = lax.broadcasted_iota(jnp.int32, (256, 128), 0)
    column = lax.broadcasted_iota(jnp.int32, (256, 128), 1)
    own = (row // 128) == ((column // 4) % 2)
    down = jnp.where(own, down, 0.0).astype(jnp.bfloat16)
    back = jnp.where(own, adapter_scale * back, 0.0).astype(jnp.bfloat16)
    back_ref[...] = back
    over_rows = (((0,), (0,)), ((), ()))
    for j in range(8):
        u, v = j % 4, j // 4
        part = lax.dot_general(
            back,
            token_columns(j),
            over_rows,
            preferred_element_type=jnp.float32,
        ) * (1.0 / BLOCK_LENGTH)
        up = lax.dot_general(
            down, grad_columns(j), over_rows, preferred_element_type=jnp.float32
        ) * (adapter_scale / BLOCK_LENGTH)
        piece = [part[:, 128 * k : 128 * k + 128] for k in range(5)]
        turned = [None, None] + [pltpu.roll(t, 64, 1) for t in piece[2:]]
        up_turned = pltpu.roll(up, 64, 1)
        out = [
            piece[0],
            piece[1],
            jnp.where(low, piece[2], up_turned),
            jnp.where(low, turned[2], turned[3]),
            jnp.where(low, turned[3], turned[4]),
            jnp.where(low, turned[4], up),
        ]
        for c in range(2):
            for k in range(3):
                at = u * GROUP + 128 * k
                terms_ref[2 * v + c, :, at : at + 128] = out[3 * c + k].astype(jnp.bfloat16)


def input_kernel(live_ref, cotangent_ref, back_ref, wide_ref, weight_ref, out_ref, grads):
    @pl.when(pl.program_id(0) == 0)
    def _():
        grads[...] = masked_rows(live_ref, cotangent_ref)

    low_rank = jnp.dot(back_ref[...], wide_ref[0], preferred_element_type=jnp.float32)
    low_rank = low_rank.astype(jnp.bfloat16).astype(jnp.float32)
    weight = weight_ref[...].reshape(640, 1024)
    frozen = lax.dot_general(
        grads[...], weight, (((1,), (1,)), ((), ())), preferred_element_type=jnp.float32
    )
    out_ref[...] = (frozen + low_rank).astype(jnp.bfloat16)


def on_device(
    tokens,
    cotangent,
    block_adapter,
    live_length,
    storage_row_of_adapter,
    value_weight,
    adapter_down_weight,
    adapter_up_weight,
):
    bf16, f32 = jnp.bfloat16, jnp.float32
    named = block_adapter[:, :1] == jnp.arange(64, dtype=jnp.int32)[None, :]
    block_slots = jnp.sum(jnp.where(named, storage_row_of_adapter[None, :], 0), axis=1)
    slot_row = jnp.pad(block_slots.astype(bf16), (0, 126))
    own = jnp.concatenate(
        [jnp.transpose(adapter_down_weight, (0, 2, 1)), adapter_up_weight], axis=2
    )
    own = jnp.transpose(own.reshape(4, 16, 4, GROUP), (1, 0, 2, 3)).reshape(16, 16, GROUP)
    own = jnp.concatenate([own, jnp.broadcast_to(slot_row, (16, 16, 128))], axis=2)
    first = lax.all_to_all(own, DP, split_axis=0, concat_axis=0, tiled=True)
    table = first[:, :, :GROUP].reshape(256, GROUP)

    tables = [table] + [lax.ppermute(table, COLUMN, HEAR[k]) for k in (1, 2, 3)]

    near = jnp.pad(first[:, 0, GROUP : GROUP + 2].astype(jnp.int32).reshape(1, 32), ((0, 0), (0, 96)))
    swap = [(0, 1), (1, 0)]
    seen = jnp.concatenate(
        [
            near,
            lax.ppermute(near, "c", swap),
            lax.ppermute(near, "v", swap),
            lax.ppermute(near, ("v", "c"), [(i, 3 - i) for i in range(4)]),
        ],
        axis=0,
    )
    place = lax.axis_index("v") * 2 + lax.axis_index("c")
    index = jnp.arange(4, dtype=jnp.int32)
    match = (index[:, None] ^ index[None, :]) == place
    cell_slots = jnp.sum(jnp.where(match[:, :, None], seen[None, :, :32], 0), axis=1)
    target = (cell_slots.reshape(128, 1) * 4 + jnp.arange(4, dtype=jnp.int32)[None, :]).reshape(512)

    chosen = pl.pallas_call(
        select_kernel,
        out_shape=jax.ShapeDtypeStruct((512, 4 * GROUP), bf16),
        compiler_params=BIG,
        name="select_rows",
    )(target.reshape(512, 1), *tables)
    maps = lax.all_to_all(
        chosen.reshape(64, 8, 4 * GROUP), CELL, split_axis=0, concat_axis=0, tiled=True
    ).reshape(4, 128, 4 * GROUP)

    smem = pl.BlockSpec(memory_space=pltpu.SMEM)
    vmem = pl.BlockSpec(memory_space=pltpu.VMEM)
    terms, back, wide = pl.pallas_call(
        block_kernel,
        out_shape=(
            jax.ShapeDtypeStruct((4, 128, 4 * GROUP), bf16),
            jax.ShapeDtypeStruct((256, 128), bf16),
            jax.ShapeDtypeStruct((8, 128, 640), bf16),
        ),
        in_specs=[smem, smem, vmem, vmem, vmem],
        scratch_shapes=[pltpu.VMEM((256, 1024), bf16)],
        compiler_params=BIG,
        cost_estimate=pl.CostEstimate(flops=10**9, bytes_accessed=9 * 10**6, transcendentals=0),
        name="block_terms",
    )(lax.axis_index("u").astype(jnp.int32).reshape(1), live_length, tokens, cotangent, maps)

    returned = lax.all_to_all(
        terms.reshape(64, 8, 4 * GROUP), CELL, split_axis=0, concat_axis=0, tiled=True
    ).reshape(512, 4 * GROUP)
    sums = pl.pallas_call(
        collect_kernel,
        out_shape=(jax.ShapeDtypeStruct((256, GROUP), f32),)
        + (jax.ShapeDtypeStruct((256, GROUP), bf16),) * 3,
        compiler_params=BIG,
        name="collect_rows",
    )(target.reshape(1, 512), returned)
    parts = [sums[0]] + [lax.ppermute(sums[k], COLUMN, TELL[k]) for k in (1, 2, 3)]
    half = lax.all_gather(value_weight, COLUMN, axis=0, tiled=False)
    half, _ = lax.optimization_barrier((half, maps))
    weight = lax.all_gather(half, "c", axis=0, tiled=False)
    weight, _ = lax.optimization_barrier((weight, sums[1]))
    input_grad = pl.pallas_call(
        input_kernel,
        grid=(8,),
        out_shape=jax.ShapeDtypeStruct((256, 5120), bf16),
        in_specs=[
            smem,
            pl.BlockSpec((256, 1024), lambda j: (0, 0)),
            pl.BlockSpec((256, 128), lambda j: (0, 0)),
            pl.BlockSpec((1, 128, 640), lambda j: (j, 0, 0)),
            pl.BlockSpec((2, 1, 320, 1024), lambda j: (0, j, 0, 0)),
        ],
        out_specs=pl.BlockSpec((256, 640), lambda j: (0, j)),
        scratch_shapes=[pltpu.VMEM((256, 1024), bf16)],
        compiler_params=pltpu.CompilerParams(vmem_limit_bytes=56 * 1024 * 1024),
        cost_estimate=pl.CostEstimate(
            flops=3 * 10**9, bytes_accessed=16 * 10**6, transcendentals=0
        ),
        name="input_grad",
    )(live_length, cotangent, back, wide, weight)
    parts[3], input_grad = lax.optimization_barrier((parts[3], input_grad))
    merged = pl.pallas_call(
        merge_kernel,
        out_shape=jax.ShapeDtypeStruct((256, GROUP), f32),
        compiler_params=BIG,
        name="merge_sums",
    )(*parts)
    parts = lax.all_to_all(
        merged.reshape(16, 16, GROUP), DP, split_axis=0, concat_axis=0, tiled=True
    )
    down, grad_up = pl.pallas_call(
        finish_kernel,
        out_shape=(
            jax.ShapeDtypeStruct((4, 64, 320), f32),
            jax.ShapeDtypeStruct((4, 64, 64), f32),
        ),
        compiler_params=BIG,
        name="finish_sums",
    )(parts)
    grad_down = jnp.transpose(down, (0, 2, 1))

    return (input_grad, grad_down, grad_up)


def solution(mesh):
    fine = Mesh(mesh.devices.reshape(4, 4, 4, 2, 2), EVERY)
    placed = (
        P(EVERY, None),
        P(EVERY, None),
        P(EVERY, None),
        P(EVERY),
        P(),
        P(FSDP, None),
        P(DP, FSDP, None),
        P(DP, None, FSDP),
    )
    return jax.shard_map(
        on_device,
        mesh=fine,
        in_specs=placed,
        out_specs=(P(EVERY, None), P(DP, FSDP, None), P(DP, None, FSDP)),
        check_vma=False,
    )
```

```python
import jax
import jax.numpy as jnp
from jax import lax
from jax.experimental import pallas as pl
from jax.experimental.pallas import tpu as pltpu
from jax.sharding import Mesh
from jax.sharding import PartitionSpec as P

BLOCK_LENGTH = 128
adapter_scale = 2.0

EVERY = ("x", "y", "u", "v", "c")
DP = ("x", "y")
COLUMN = ("u", "v")
FSDP = ("u", "v", "c")
CELL = ("v", "c", "x", "y")
HEAR = [[((z - k) % 8 if z % 2 == 0 else (z + k) % 8, z) for z in range(8)] for k in range(4)]
TELL = [[(b, a) for a, b in pairs] for pairs in HEAR]
GROUP = 384
BIG = pltpu.CompilerParams(vmem_limit_bytes=20 * 1024 * 1024)


def pack_kernel(
    near_ref, core_ref, level_ref, both_ref, down_hbm, up_hbm, out_ref, down_ref, up_ref, sems
):
    f32, bf16 = jnp.float32, jnp.bfloat16
    copies = [
        pltpu.make_async_copy(down_hbm, down_ref, sems.at[0]),
        pltpu.make_async_copy(up_hbm, up_ref, sems.at[1]),
    ]
    for copy in copies:
        copy.start()
    line = lax.broadcasted_iota(jnp.int32, (16, 128), 0)
    slots = jnp.zeros((16, 128), jnp.int32)
    for i, ref in enumerate((near_ref, core_ref, level_ref, both_ref)):
        slots = jnp.where(line == i, jnp.broadcast_to(ref[...], (16, 128)), slots)
    slots = slots.astype(f32).astype(bf16)
    for copy in copies:
        copy.wait()
    maps = [
        jnp.concatenate([down_ref[s].astype(f32), up_ref[s].astype(f32)], axis=1) for s in range(4)
    ]
    for d in range(16):
        rows = jnp.concatenate([m[4 * d : 4 * d + 4] for m in maps], axis=0)
        out_ref[d, :, :GROUP] = rows.astype(bf16)
        out_ref[d, :, GROUP:] = slots


def mask_kernel(live_ref, cotangent_ref, grads_ref):
    grads_ref[...] = masked_rows(live_ref, cotangent_ref)


def select_kernel(target_ref, table0, table1, table2, table3, out_ref):
    rows = out_ref.shape[0]
    lane = lax.broadcasted_iota(jnp.int32, (rows, 256), 1)
    pick = jnp.where(lane == target_ref[...], 1.0, 0.0).astype(jnp.bfloat16)
    for k, table in enumerate((table0, table1, table2, table3)):
        part = jnp.dot(pick, table[...], preferred_element_type=jnp.float32)
        out_ref[:, k * GROUP : (k + 1) * GROUP] = part.astype(jnp.bfloat16)


def collect_kernel(target_ref, terms_ref, out0, out1, out2, out3):
    rows = terms_ref.shape[0]
    sub = lax.broadcasted_iota(jnp.int32, (256, rows), 0)
    pick = jnp.where(sub == target_ref[...], 1.0, 0.0).astype(jnp.bfloat16)
    for k, out in enumerate((out0, out1, out2, out3)):
        part = jnp.dot(
            pick, terms_ref[:, k * GROUP : (k + 1) * GROUP], preferred_element_type=jnp.float32
        )
        out[...] = part.astype(out.dtype)


def merge_kernel(part0, part1, part2, part3, out_ref):
    f32 = jnp.float32
    out_ref[...] = (part0[...] + part1[...].astype(f32)) + (
        part2[...].astype(f32) + part3[...].astype(f32)
    )


def finish_kernel(parts_ref, down_ref, up_ref):
    for d in range(16):
        for s in range(4):
            rows = parts_ref[d, 4 * s : 4 * s + 4, :]
            down_ref[s, 4 * d : 4 * d + 4, :] = rows[:, :320]
            up_ref[s, 4 * d : 4 * d + 4, :] = rows[:, 320:]


def masked_rows(live_ref, cotangent_ref):
    count = cotangent_ref.shape[0]
    row = lax.broadcasted_iota(jnp.int32, (count, 1), 0)
    limit = jnp.where(row < BLOCK_LENGTH, live_ref[0], live_ref[1] + BLOCK_LENGTH)
    grads = cotangent_ref[...]
    return jnp.where(row < limit, grads, jnp.zeros_like(grads))


def shard_of(cell, j):
    z = cell * 2 + (8 - j if j < 4 else 1 + j - 4)
    return lax.rem(z, 8)


def block_kernel(
    cell_ref,
    tokens_ref,
    grads,
    maps_ref,
    terms_ref,
    back_out,
    wide_out,
    back_ref,
    wide_ref,
    back_sem,
    wide_sems,
):
    f32, bf16 = jnp.float32, jnp.bfloat16
    shards = [shard_of(cell_ref[0], j) for j in range(8)]
    leaving = []

    def send(source, target, sem):
        copy = pltpu.make_async_copy(source, target, sem)
        copy.start()
        leaving.append(copy)

    def token_columns(j):
        return tokens_ref[:, pl.ds(pl.multiple_of(shards[j] * 640, 128), 640)]

    def grad_columns(j):
        return grads[:, pl.ds(pl.multiple_of(shards[j] * 128, 128), 128)]

    low = lax.broadcasted_iota(jnp.int32, (128, 128), 1) < 64
    contract = (((1,), (1,)), ((), ()))
    over_rows = (((0,), (0,)), ((), ()))
    row = lax.broadcasted_iota(jnp.int32, (256, 128), 0)
    column = lax.broadcasted_iota(jnp.int32, (256, 128), 1)
    own = (row // 128) == ((column // 4) % 2)

    back = jnp.zeros((256, 128), f32)
    for j in range(8):
        k, v = j % 4, j // 4
        tiles = [
            maps_ref[2 * v + c, :, k * GROUP + 128 * i : k * GROUP + 128 * i + 128].astype(f32)
            for c in range(2)
            for i in range(3)
        ]
        turned = [None, None] + [pltpu.roll(t, 64, 1) for t in tiles[2:]]
        wide = [
            tiles[0],
            tiles[1],
            jnp.where(low, tiles[2], turned[3]),
            jnp.where(low, turned[3], turned[4]),
            jnp.where(low, turned[4], turned[5]),
        ]
        wide_ref[j] = jnp.concatenate(wide, axis=1).astype(bf16)
        send(wide_ref.at[j], wide_out.at[shards[j]], wide_sems.at[j])
        up = jnp.where(low, turned[2], tiles[5]).astype(bf16)
        back = back + lax.dot_general(grad_columns(j), up, contract, preferred_element_type=f32)
    back = jnp.where(own, adapter_scale * back, 0.0).astype(bf16)
    back_ref[...] = back
    send(back_ref, back_out, back_sem)

    down = jnp.zeros((256, 128), f32)
    for j in range(8):
        k, v = j % 4, j // 4
        rows = token_columns(j)
        part = lax.dot_general(back, rows, over_rows, preferred_element_type=f32)
        part = part * (1.0 / BLOCK_LENGTH)
        down = down + lax.dot_general(rows, wide_ref[j], contract, preferred_element_type=f32)
        piece = [part[:, 128 * i : 128 * i + 128] for i in range(5)]
        turned = [None, None] + [pltpu.roll(t, 64, 1) for t in piece[2:]]
        out = [
            piece[0],
            piece[1],
            piece[2],
            jnp.where(low, turned[2], turned[3]),
            jnp.where(low, turned[3], turned[4]),
            turned[4],
        ]
        for c in range(2):
            for i in range(3):
                at = k * GROUP + 128 * i
                terms_ref[2 * v + c, :, at : at + 128] = out[3 * c + i].astype(bf16)
    down = jnp.where(own, down, 0.0).astype(bf16)
    for j in range(8):
        k, v = j % 4, j // 4
        up = lax.dot_general(down, grad_columns(j), over_rows, preferred_element_type=f32)
        up = up * (adapter_scale / BLOCK_LENGTH)
        for c, value in enumerate((pltpu.roll(up, 64, 1), up)):
            at = slice(k * GROUP + 256, k * GROUP + 384)
            kept = terms_ref[2 * v + c, :, at]
            terms_ref[2 * v + c, :, at] = jnp.where(low, kept, value.astype(bf16))
    for copy in leaving:
        copy.wait()


def met_at(k, where_ref):
    return jnp.where(k < 4, k, 11 - k) ^ where_ref[1]


def input_kernel(where_ref, masked_ref, back_ref, wide_ref, own_ref, other_ref, out_ref, weight):
    low_rank = jnp.dot(back_ref[...], wide_ref[0], preferred_element_type=jnp.float32)
    low_rank = low_rank.astype(jnp.bfloat16).astype(jnp.float32)
    core = where_ref[0]
    for start, source in ((core * 320, own_ref), (320 - core * 320, other_ref)):
        for d in range(16):
            rows = pl.ds(pl.multiple_of(start + d // 4 * 80, 80), 80)
            columns = slice(d % 4 * 256, d % 4 * 256 + 256)
            weight[rows, columns] = source[d, 0]
    frozen = lax.dot_general(
        masked_ref[...], weight[...], (((1,), (1,)), ((), ())), preferred_element_type=jnp.float32
    )
    out_ref[...] = (frozen + low_rank).astype(jnp.bfloat16)


def on_device(
    tokens,
    cotangent,
    block_adapter,
    live_length,
    storage_row_of_adapter,
    value_weight,
    adapter_down_weight,
    adapter_up_weight,
):
    bf16, f32 = jnp.bfloat16, jnp.float32
    x, y = lax.axis_index("x"), lax.axis_index("y")
    pieces = lax.dynamic_slice(value_weight, (x * 80, y * 256), (80, 256))[None]
    for m in (1, 2, 7):
        met = lax.ppermute(pieces, COLUMN, [(z, z ^ m) for z in range(8)])
        pieces = jnp.concatenate([pieces, met], axis=0)

    named = block_adapter[:, :1] == jnp.arange(64, dtype=jnp.int32)[None, :]
    near = jnp.sum(jnp.where(named, storage_row_of_adapter[None, :], 0), axis=1)
    near = jnp.pad(near, (0, 126))[None]
    swap = [(0, 1), (1, 0)]
    seen = [
        near,
        lax.ppermute(near, "c", swap),
        lax.ppermute(near, "v", swap),
        lax.ppermute(near, ("v", "c"), [(i, 3 - i) for i in range(4)]),
    ]

    smem = pl.BlockSpec(memory_space=pltpu.SMEM)
    vmem = pl.BlockSpec(memory_space=pltpu.VMEM)
    hbm = pl.BlockSpec(memory_space=pltpu.HBM)
    in_hbm = lambda x: pltpu.with_memory_space_constraint(x, pltpu.HBM)
    own = pl.pallas_call(
        pack_kernel,
        out_shape=pltpu.HBM((16, 16, GROUP + 128), bf16),
        in_specs=[vmem, vmem, vmem, vmem, hbm, hbm],
        out_specs=vmem,
        scratch_shapes=[
            pltpu.VMEM((4, 64, 320), bf16),
            pltpu.VMEM((4, 64, 64), bf16),
            pltpu.SemaphoreType.DMA((2,)),
        ],
        compiler_params=BIG,
        name="pack_maps",
    )(
        *seen,
        in_hbm(jnp.transpose(adapter_down_weight, (0, 2, 1))),
        in_hbm(adapter_up_weight),
    )
    first = lax.all_to_all(own, DP, split_axis=0, concat_axis=0, tiled=True)
    table = first[:, :, :GROUP].reshape(256, GROUP)

    tables = [table] + [lax.ppermute(table, COLUMN, HEAR[k]) for k in (1, 2, 3)]

    seen = first[:, :4, GROUP : GROUP + 2].astype(jnp.int32)
    place = lax.axis_index("v") * 2 + lax.axis_index("c")
    index = jnp.arange(4, dtype=jnp.int32)
    match = (index[:, None] ^ index[None, :]) == place
    cell_slots = jnp.sum(jnp.where(match[:, None, :, None], seen[None], 0), axis=2)
    target = (cell_slots.reshape(128, 1) * 4 + jnp.arange(4, dtype=jnp.int32)[None, :]).reshape(512)

    live, _ = lax.optimization_barrier((live_length, table))
    masked = pl.pallas_call(
        mask_kernel,
        out_shape=pltpu.VMEM((256, 1024), bf16),
        in_specs=[smem, vmem],
        out_specs=vmem,
        compiler_params=BIG,
        name="mask_rows",
    )(live, cotangent)
    target_row = target.reshape(1, 512)
    cell = lax.axis_index("u").astype(jnp.int32).reshape(1)
    tables, masked, target_row, cell = lax.optimization_barrier((tables, masked, target_row, cell))
    pieces, _ = lax.optimization_barrier((pieces, table))
    half = lax.all_gather(pieces, DP, axis=0, tiled=False)

    chosen = pl.pallas_call(
        select_kernel,
        out_shape=jax.ShapeDtypeStruct((512, 4 * GROUP), bf16),
        compiler_params=BIG,
        name="select_rows",
    )(target.reshape(512, 1), *tables)
    maps = lax.all_to_all(
        chosen.reshape(64, 8, 4 * GROUP), CELL, split_axis=0, concat_axis=0, tiled=True
    ).reshape(4, 128, 4 * GROUP)

    terms, back, wide = pl.pallas_call(
        block_kernel,
        out_shape=(
            jax.ShapeDtypeStruct((4, 128, 4 * GROUP), bf16),
            pltpu.HBM((256, 128), bf16),
            pltpu.HBM((8, 128, 640), bf16),
        ),
        in_specs=[smem, vmem, vmem, vmem],
        out_specs=(vmem, hbm, hbm),
        scratch_shapes=[
            pltpu.VMEM((256, 128), bf16),
            pltpu.VMEM((8, 128, 640), bf16),
            pltpu.SemaphoreType.DMA,
            pltpu.SemaphoreType.DMA((8,)),
        ],
        compiler_params=BIG,
        cost_estimate=pl.CostEstimate(flops=10**9, bytes_accessed=9 * 10**6, transcendentals=0),
        name="block_terms",
    )(cell, tokens, masked, maps)

    returned = lax.all_to_all(
        terms.reshape(64, 8, 4 * GROUP), CELL, split_axis=0, concat_axis=0, tiled=True
    ).reshape(512, 4 * GROUP)
    sums = pl.pallas_call(
        collect_kernel,
        out_shape=(jax.ShapeDtypeStruct((256, GROUP), f32),)
        + (jax.ShapeDtypeStruct((256, GROUP), bf16),) * 3,
        compiler_params=BIG,
        name="collect_rows",
    )(target_row, returned)
    parts = [sums[0]] + [lax.ppermute(sums[k], COLUMN, TELL[k]) for k in (1, 2, 3)]
    half, _ = lax.optimization_barrier((half, sums[1]))
    other = lax.ppermute(half, "c", [(0, 1), (1, 0)])
    where = jnp.stack(
        [lax.axis_index("c"), lax.axis_index("u") * 2 + lax.axis_index("v")]
    ).astype(jnp.int32)
    weight_block = pl.BlockSpec((16, 1, 80, 256), lambda k, w: (0, k, 0, 0))
    input_grad = pl.pallas_call(
        input_kernel,
        out_shape=jax.ShapeDtypeStruct((256, 5120), bf16),
        grid_spec=pltpu.PrefetchScalarGridSpec(
            num_scalar_prefetch=1,
            grid=(8,),
            in_specs=[
                pl.BlockSpec((256, 1024), lambda k, w: (0, 0)),
                pl.BlockSpec((256, 128), lambda k, w: (0, 0)),
                pl.BlockSpec((1, 128, 640), lambda k, w: (met_at(k, w), 0, 0)),
                weight_block,
                weight_block,
            ],
            out_specs=pl.BlockSpec((256, 640), lambda k, w: (0, met_at(k, w))),
            scratch_shapes=[pltpu.VMEM((640, 1024), bf16)],
        ),
        compiler_params=BIG,
        cost_estimate=pl.CostEstimate(
            flops=3 * 10**9, bytes_accessed=16 * 10**6, transcendentals=0
        ),
        name="input_grad",
    )(where, masked, back, wide, in_hbm(half), other)
    parts[3], input_grad = lax.optimization_barrier((parts[3], input_grad))
    merged = pl.pallas_call(
        merge_kernel,
        out_shape=jax.ShapeDtypeStruct((256, GROUP), f32),
        compiler_params=BIG,
        name="merge_sums",
    )(*parts)
    parts = lax.all_to_all(
        merged.reshape(16, 16, GROUP), DP, split_axis=0, concat_axis=0, tiled=True
    )
    down, grad_up = pl.pallas_call(
        finish_kernel,
        out_shape=(
            jax.ShapeDtypeStruct((4, 64, 320), f32),
            jax.ShapeDtypeStruct((4, 64, 64), f32),
        ),
        compiler_params=BIG,
        name="finish_sums",
    )(parts)
    grad_down = jnp.transpose(down, (0, 2, 1))

    return (input_grad, grad_down, grad_up)


def solution(mesh):
    fine = Mesh(mesh.devices.reshape(4, 4, 4, 2, 2), EVERY)
    placed = (
        P(EVERY, None),
        P(EVERY, None),
        P(EVERY, None),
        P(EVERY),
        P(),
        P(FSDP, None),
        P(DP, FSDP, None),
        P(DP, None, FSDP),
    )
    return jax.shard_map(
        on_device,
        mesh=fine,
        in_specs=placed,
        out_specs=(P(EVERY, None), P(DP, FSDP, None), P(DP, None, FSDP)),
        check_vma=False,
    )
```

```python
import jax
import jax.numpy as jnp
from jax import lax
from jax.experimental import pallas as pl
from jax.experimental.pallas import tpu as pltpu
from jax.sharding import Mesh
from jax.sharding import PartitionSpec as P

BLOCK_LENGTH = 128
adapter_scale = 2.0

EVERY = ("x", "y", "u", "v", "c")
DP = ("x", "y")
COLUMN = ("u", "v")
FSDP = ("u", "v", "c")
CELL = ("v", "c", "x", "y")
HEAR = [[((z - k) % 8 if z % 2 == 0 else (z + k) % 8, z) for z in range(8)] for k in range(4)]
TELL = [[(b, a) for a, b in pairs] for pairs in HEAR]
GROUP = 384
BIG = pltpu.CompilerParams(vmem_limit_bytes=20 * 1024 * 1024)


def pack_kernel(
    near_ref, core_ref, level_ref, both_ref, down_hbm, up_hbm, out_ref, down_ref, up_ref, sems
):
    f32, bf16 = jnp.float32, jnp.bfloat16
    copies = [
        pltpu.make_async_copy(down_hbm, down_ref, sems.at[0]),
        pltpu.make_async_copy(up_hbm, up_ref, sems.at[1]),
    ]
    for copy in copies:
        copy.start()
    line = lax.broadcasted_iota(jnp.int32, (16, 128), 0)
    slots = jnp.zeros((16, 128), jnp.int32)
    for i, ref in enumerate((near_ref, core_ref, level_ref, both_ref)):
        slots = jnp.where(line == i, jnp.broadcast_to(ref[...], (16, 128)), slots)
    slots = slots.astype(f32).astype(bf16)
    for copy in copies:
        copy.wait()
    maps = [
        jnp.concatenate([down_ref[s].astype(f32), up_ref[s].astype(f32)], axis=1) for s in range(4)
    ]
    for d in range(16):
        rows = jnp.concatenate([m[4 * d : 4 * d + 4] for m in maps], axis=0)
        out_ref[d, :, :GROUP] = rows.astype(bf16)
        out_ref[d, :, GROUP:] = slots


def mask_kernel(live_ref, cotangent_ref, grads_ref):
    grads_ref[...] = masked_rows(live_ref, cotangent_ref)


def select_kernel(target_ref, table0, table1, table2, table3, out_ref):
    rows = out_ref.shape[0]
    lane = lax.broadcasted_iota(jnp.int32, (rows, 256), 1)
    pick = jnp.where(lane == target_ref[...], 1.0, 0.0).astype(jnp.bfloat16)
    for k, table in enumerate((table0, table1, table2, table3)):
        part = jnp.dot(pick, table[...], preferred_element_type=jnp.float32)
        out_ref[:, k * GROUP : (k + 1) * GROUP] = part.astype(jnp.bfloat16)


def collect_kernel(target_ref, terms_ref, out0, out1, out2, out3):
    rows = terms_ref.shape[0]
    sub = lax.broadcasted_iota(jnp.int32, (256, rows), 0)
    pick = jnp.where(sub == target_ref[...], 1.0, 0.0).astype(jnp.bfloat16)
    for k, out in enumerate((out0, out1, out2, out3)):
        part = jnp.dot(
            pick, terms_ref[:, k * GROUP : (k + 1) * GROUP], preferred_element_type=jnp.float32
        )
        out[...] = part.astype(out.dtype)


def merge_kernel(part0, part1, part2, part3, out_ref):
    f32 = jnp.float32
    out_ref[...] = (part0[...] + part1[...].astype(f32)) + (
        part2[...].astype(f32) + part3[...].astype(f32)
    )


def finish_kernel(parts_ref, down_ref, up_ref):
    for d in range(16):
        for s in range(4):
            rows = parts_ref[d, 4 * s : 4 * s + 4, :]
            down_ref[s, 4 * d : 4 * d + 4, :] = rows[:, :320]
            up_ref[s, 4 * d : 4 * d + 4, :] = rows[:, 320:]


def masked_rows(live_ref, cotangent_ref):
    count = cotangent_ref.shape[0]
    row = lax.broadcasted_iota(jnp.int32, (count, 1), 0)
    limit = jnp.where(row < BLOCK_LENGTH, live_ref[0], live_ref[1] + BLOCK_LENGTH)
    grads = cotangent_ref[...]
    return jnp.where(row < limit, grads, jnp.zeros_like(grads))


def shard_of(cell, j):
    z = cell * 2 + (8 - j if j < 4 else 1 + j - 4)
    return lax.rem(z, 8)


def block_kernel(
    cell_ref,
    tokens_ref,
    grads,
    maps_ref,
    terms_ref,
    back_out,
    wide_out,
    back_ref,
    wide_ref,
    back_sem,
    wide_sems,
):
    f32, bf16 = jnp.float32, jnp.bfloat16
    shards = [shard_of(cell_ref[0], j) for j in range(8)]
    leaving = []

    def send(source, target, sem):
        copy = pltpu.make_async_copy(source, target, sem)
        copy.start()
        leaving.append(copy)

    def token_columns(j):
        return tokens_ref[:, pl.ds(pl.multiple_of(shards[j] * 640, 128), 640)]

    def grad_columns(j):
        return grads[:, pl.ds(pl.multiple_of(shards[j] * 128, 128), 128)]

    low = lax.broadcasted_iota(jnp.int32, (128, 128), 1) < 64
    contract = (((1,), (1,)), ((), ()))
    over_rows = (((0,), (0,)), ((), ()))
    row = lax.broadcasted_iota(jnp.int32, (256, 128), 0)
    column = lax.broadcasted_iota(jnp.int32, (256, 128), 1)
    own = (row // 128) == ((column // 4) % 2)

    back = jnp.zeros((256, 128), f32)
    for j in range(8):
        k, v = j % 4, j // 4
        tiles = [
            maps_ref[2 * v + c, :, k * GROUP + 128 * i : k * GROUP + 128 * i + 128].astype(f32)
            for c in range(2)
            for i in range(3)
        ]
        turned = [None, None] + [pltpu.roll(t, 64, 1) for t in tiles[2:]]
        wide = [
            tiles[0],
            tiles[1],
            jnp.where(low, tiles[2], turned[3]),
            jnp.where(low, turned[3], turned[4]),
            jnp.where(low, turned[4], turned[5]),
        ]
        wide_ref[j] = jnp.concatenate(wide, axis=1).astype(bf16)
        send(wide_ref.at[j], wide_out.at[shards[j]], wide_sems.at[j])
        up = jnp.where(low, turned[2], tiles[5]).astype(bf16)
        back = back + lax.dot_general(grad_columns(j), up, contract, preferred_element_type=f32)
    back = jnp.where(own, adapter_scale * back, 0.0).astype(bf16)
    back_ref[...] = back
    send(back_ref, back_out, back_sem)

    down = jnp.zeros((256, 128), f32)
    for j in range(8):
        k, v = j % 4, j // 4
        rows = token_columns(j)
        part = lax.dot_general(back, rows, over_rows, preferred_element_type=f32)
        part = part * (1.0 / BLOCK_LENGTH)
        down = down + lax.dot_general(rows, wide_ref[j], contract, preferred_element_type=f32)
        piece = [part[:, 128 * i : 128 * i + 128] for i in range(5)]
        turned = [None, None] + [pltpu.roll(t, 64, 1) for t in piece[2:]]
        out = [
            piece[0],
            piece[1],
            piece[2],
            jnp.where(low, turned[2], turned[3]),
            jnp.where(low, turned[3], turned[4]),
            turned[4],
        ]
        for c in range(2):
            for i in range(3):
                at = k * GROUP + 128 * i
                terms_ref[2 * v + c, :, at : at + 128] = out[3 * c + i].astype(bf16)
    down = jnp.where(own, down, 0.0).astype(bf16)
    for j in range(8):
        k, v = j % 4, j // 4
        up = lax.dot_general(down, grad_columns(j), over_rows, preferred_element_type=f32)
        up = up * (adapter_scale / BLOCK_LENGTH)
        for c, value in enumerate((pltpu.roll(up, 64, 1), up)):
            at = slice(k * GROUP + 256, k * GROUP + 384)
            kept = terms_ref[2 * v + c, :, at]
            terms_ref[2 * v + c, :, at] = jnp.where(low, kept, value.astype(bf16))
    for copy in leaving:
        copy.wait()


def met_at(k, where_ref):
    return ((k & 1) * 7) ^ (k & 2) ^ (k >> 2) ^ where_ref[1]


def input_kernel(where_ref, masked_ref, back_ref, wide_ref, own_ref, other_ref, out_ref, weight):
    low_rank = jnp.dot(back_ref[...], wide_ref[0], preferred_element_type=jnp.float32)
    low_rank = low_rank.astype(jnp.bfloat16).astype(jnp.float32)
    core = where_ref[0]
    for start, source in ((core * 320, own_ref), (320 - core * 320, other_ref)):
        for d in range(16):
            rows = pl.ds(pl.multiple_of(start + d // 4 * 80, 80), 80)
            columns = slice(d % 4 * 256, d % 4 * 256 + 256)
            weight[rows, columns] = source[d, 0]
    frozen = lax.dot_general(
        masked_ref[...], weight[...], (((1,), (1,)), ((), ())), preferred_element_type=jnp.float32
    )
    out_ref[...] = (frozen + low_rank).astype(jnp.bfloat16)


def double(pieces, m):
    met = lax.ppermute(pieces, COLUMN, [(z, z ^ m) for z in range(8)])
    return jnp.concatenate([pieces, met], axis=0)


def on_device(
    tokens,
    cotangent,
    block_adapter,
    live_length,
    storage_row_of_adapter,
    value_weight,
    adapter_down_weight,
    adapter_up_weight,
):
    bf16, f32 = jnp.bfloat16, jnp.float32
    x, y = lax.axis_index("x"), lax.axis_index("y")
    pieces = lax.dynamic_slice(value_weight, (x * 80, y * 256), (80, 256))[None]
    pieces = double(pieces, 7)

    named = block_adapter[:, :1] == jnp.arange(64, dtype=jnp.int32)[None, :]
    near = jnp.sum(jnp.where(named, storage_row_of_adapter[None, :], 0), axis=1)
    near = jnp.pad(near, (0, 126))[None]
    swap = [(0, 1), (1, 0)]
    seen = [
        near,
        lax.ppermute(near, "c", swap),
        lax.ppermute(near, "v", swap),
        lax.ppermute(near, ("v", "c"), [(i, 3 - i) for i in range(4)]),
    ]

    smem = pl.BlockSpec(memory_space=pltpu.SMEM)
    vmem = pl.BlockSpec(memory_space=pltpu.VMEM)
    hbm = pl.BlockSpec(memory_space=pltpu.HBM)
    in_hbm = lambda x: pltpu.with_memory_space_constraint(x, pltpu.HBM)
    own = pl.pallas_call(
        pack_kernel,
        out_shape=pltpu.HBM((16, 16, GROUP + 128), bf16),
        in_specs=[vmem, vmem, vmem, vmem, hbm, hbm],
        out_specs=vmem,
        scratch_shapes=[
            pltpu.VMEM((4, 64, 320), bf16),
            pltpu.VMEM((4, 64, 64), bf16),
            pltpu.SemaphoreType.DMA((2,)),
        ],
        compiler_params=BIG,
        name="pack_maps",
    )(
        *seen,
        in_hbm(jnp.transpose(adapter_down_weight, (0, 2, 1))),
        in_hbm(adapter_up_weight),
    )
    pieces, _ = lax.optimization_barrier((pieces, own))
    pieces = double(double(pieces, 2), 1)
    first = lax.all_to_all(own, DP, split_axis=0, concat_axis=0, tiled=True)
    table = first[:, :, :GROUP].reshape(256, GROUP)

    tables = [table] + [lax.ppermute(table, COLUMN, HEAR[k]) for k in (1, 2, 3)]

    seen = first[:, :4, GROUP : GROUP + 2].astype(jnp.int32)
    place = lax.axis_index("v") * 2 + lax.axis_index("c")
    index = jnp.arange(4, dtype=jnp.int32)
    match = (index[:, None] ^ index[None, :]) == place
    cell_slots = jnp.sum(jnp.where(match[:, None, :, None], seen[None], 0), axis=2)
    target = (cell_slots.reshape(128, 1) * 4 + jnp.arange(4, dtype=jnp.int32)[None, :]).reshape(512)

    live, _ = lax.optimization_barrier((live_length, table))
    masked = pl.pallas_call(
        mask_kernel,
        out_shape=pltpu.VMEM((256, 1024), bf16),
        in_specs=[smem, vmem],
        out_specs=vmem,
        compiler_params=BIG,
        name="mask_rows",
    )(live, cotangent)
    target_row = target.reshape(1, 512)
    cell = lax.axis_index("u").astype(jnp.int32).reshape(1)
    tables, masked, target_row, cell = lax.optimization_barrier((tables, masked, target_row, cell))
    pieces, _ = lax.optimization_barrier((pieces, table))
    half = lax.all_gather(pieces, DP, axis=0, tiled=False)

    chosen = pl.pallas_call(
        select_kernel,
        out_shape=jax.ShapeDtypeStruct((512, 4 * GROUP), bf16),
        compiler_params=BIG,
        name="select_rows",
    )(target.reshape(512, 1), *tables)
    maps = lax.all_to_all(
        chosen.reshape(64, 8, 4 * GROUP), CELL, split_axis=0, concat_axis=0, tiled=True
    ).reshape(4, 128, 4 * GROUP)

    terms, back, wide = pl.pallas_call(
        block_kernel,
        out_shape=(
            jax.ShapeDtypeStruct((4, 128, 4 * GROUP), bf16),
            pltpu.HBM((256, 128), bf16),
            pltpu.HBM((8, 128, 640), bf16),
        ),
        in_specs=[smem, vmem, vmem, vmem],
        out_specs=(vmem, hbm, hbm),
        scratch_shapes=[
            pltpu.VMEM((256, 128), bf16),
            pltpu.VMEM((8, 128, 640), bf16),
            pltpu.SemaphoreType.DMA,
            pltpu.SemaphoreType.DMA((8,)),
        ],
        compiler_params=BIG,
        cost_estimate=pl.CostEstimate(flops=10**9, bytes_accessed=9 * 10**6, transcendentals=0),
        name="block_terms",
    )(cell, tokens, masked, maps)

    returned = lax.all_to_all(
        terms.reshape(64, 8, 4 * GROUP), CELL, split_axis=0, concat_axis=0, tiled=True
    ).reshape(512, 4 * GROUP)
    sums = pl.pallas_call(
        collect_kernel,
        out_shape=(jax.ShapeDtypeStruct((256, GROUP), f32),)
        + (jax.ShapeDtypeStruct((256, GROUP), bf16),) * 3,
        compiler_params=BIG,
        name="collect_rows",
    )(target_row, returned)
    parts = [sums[0]] + [lax.ppermute(sums[k], COLUMN, TELL[k]) for k in (1, 2, 3)]
    half, _ = lax.optimization_barrier((half, sums[1]))
    other = lax.ppermute(half, "c", [(0, 1), (1, 0)])
    where = jnp.stack(
        [lax.axis_index("c"), lax.axis_index("u") * 2 + lax.axis_index("v")]
    ).astype(jnp.int32)
    weight_block = pl.BlockSpec((16, 1, 80, 256), lambda k, w: (0, k, 0, 0))
    input_grad = pl.pallas_call(
        input_kernel,
        out_shape=jax.ShapeDtypeStruct((256, 5120), bf16),
        grid_spec=pltpu.PrefetchScalarGridSpec(
            num_scalar_prefetch=1,
            grid=(8,),
            in_specs=[
                pl.BlockSpec((256, 1024), lambda k, w: (0, 0)),
                pl.BlockSpec((256, 128), lambda k, w: (0, 0)),
                pl.BlockSpec((1, 128, 640), lambda k, w: (met_at(k, w), 0, 0)),
                weight_block,
                weight_block,
            ],
            out_specs=pl.BlockSpec((256, 640), lambda k, w: (0, met_at(k, w))),
            scratch_shapes=[pltpu.VMEM((640, 1024), bf16)],
        ),
        compiler_params=BIG,
        cost_estimate=pl.CostEstimate(
            flops=3 * 10**9, bytes_accessed=16 * 10**6, transcendentals=0
        ),
        name="input_grad",
    )(where, masked, back, wide, in_hbm(half), other)
    parts[3], input_grad = lax.optimization_barrier((parts[3], input_grad))
    merged = pl.pallas_call(
        merge_kernel,
        out_shape=jax.ShapeDtypeStruct((256, GROUP), f32),
        compiler_params=BIG,
        name="merge_sums",
    )(*parts)
    parts = lax.all_to_all(
        merged.reshape(16, 16, GROUP), DP, split_axis=0, concat_axis=0, tiled=True
    )
    down, grad_up = pl.pallas_call(
        finish_kernel,
        out_shape=(
            jax.ShapeDtypeStruct((4, 64, 320), f32),
            jax.ShapeDtypeStruct((4, 64, 64), f32),
        ),
        compiler_params=BIG,
        name="finish_sums",
    )(parts)
    grad_down = jnp.transpose(down, (0, 2, 1))

    return (input_grad, grad_down, grad_up)


def solution(mesh):
    fine = Mesh(mesh.devices.reshape(4, 4, 4, 2, 2), EVERY)
    placed = (
        P(EVERY, None),
        P(EVERY, None),
        P(EVERY, None),
        P(EVERY),
        P(),
        P(FSDP, None),
        P(DP, FSDP, None),
        P(DP, None, FSDP),
    )
    return jax.shard_map(
        on_device,
        mesh=fine,
        in_specs=placed,
        out_specs=(P(EVERY, None), P(DP, FSDP, None), P(DP, None, FSDP)),
        check_vma=False,
    )
```

```python
import jax
import jax.numpy as jnp
from jax import lax
from jax.experimental import pallas as pl
from jax.experimental.pallas import tpu as pltpu
from jax.sharding import Mesh
from jax.sharding import PartitionSpec as P

BLOCK_LENGTH = 128
adapter_scale = 2.0

EVERY = ("x", "y", "u", "v", "c")
DP = ("x", "y")
COLUMN = ("u", "v")
FSDP = ("u", "v", "c")
CELL = ("v", "c", "x", "y")
HEAR = [[((z - k) % 8 if z % 2 == 0 else (z + k) % 8, z) for z in range(8)] for k in range(4)]
TELL = [[(b, a) for a, b in pairs] for pairs in HEAR]
GROUP = 384
BIG = pltpu.CompilerParams(vmem_limit_bytes=20 * 1024 * 1024)


def pack_kernel(down_hbm, up_hbm, out_ref, down_ref, up_ref, sems):
    f32, bf16 = jnp.float32, jnp.bfloat16
    copies = [
        pltpu.make_async_copy(down_hbm, down_ref, sems.at[0]),
        pltpu.make_async_copy(up_hbm, up_ref, sems.at[1]),
    ]
    for copy in copies:
        copy.start()
    for copy in copies:
        copy.wait()
    maps = [
        jnp.concatenate([down_ref[s].astype(f32), up_ref[s].astype(f32)], axis=1) for s in range(4)
    ]
    for d in range(16):
        rows = jnp.concatenate([m[4 * d : 4 * d + 4] for m in maps], axis=0)
        out_ref[d, :, :GROUP] = rows.astype(bf16)


def slot_kernel(near_ref, core_ref, level_ref, both_ref, packed_ref, out_ref, tile_ref, sem):
    line = lax.broadcasted_iota(jnp.int32, (16, 128), 0)
    slots = jnp.zeros((16, 128), jnp.int32)
    for i, ref in enumerate((near_ref, core_ref, level_ref, both_ref)):
        slots = jnp.where(line == i, jnp.broadcast_to(ref[...], (16, 128)), slots)
    slots = slots.astype(jnp.float32).astype(jnp.bfloat16)
    for d in range(16):
        tile_ref[d] = slots
    copy = pltpu.make_async_copy(tile_ref, out_ref.at[:, :, GROUP:], sem)
    copy.start()
    copy.wait()


def mask_kernel(live_ref, cotangent_ref, grads_ref):
    grads_ref[...] = masked_rows(live_ref, cotangent_ref)


def select_kernel(target_ref, table0, table1, table2, table3, out_ref):
    rows = out_ref.shape[0]
    lane = lax.broadcasted_iota(jnp.int32, (rows, 256), 1)
    pick = jnp.where(lane == target_ref[...], 1.0, 0.0).astype(jnp.bfloat16)
    for k, table in enumerate((table0, table1, table2, table3)):
        part = jnp.dot(pick, table[...], preferred_element_type=jnp.float32)
        out_ref[:, k * GROUP : (k + 1) * GROUP] = part.astype(jnp.bfloat16)


def collect_kernel(target_ref, terms_ref, out0, out1, out2, out3):
    rows = terms_ref.shape[0]
    sub = lax.broadcasted_iota(jnp.int32, (256, rows), 0)
    pick = jnp.where(sub == target_ref[...], 1.0, 0.0).astype(jnp.bfloat16)
    for k, out in enumerate((out0, out1, out2, out3)):
        part = jnp.dot(
            pick, terms_ref[:, k * GROUP : (k + 1) * GROUP], preferred_element_type=jnp.float32
        )
        out[...] = part.astype(out.dtype)


def merge_kernel(part0, part1, part2, part3, out_ref):
    f32 = jnp.float32
    out_ref[...] = (part0[...] + part1[...].astype(f32)) + (
        part2[...].astype(f32) + part3[...].astype(f32)
    )


def finish_kernel(parts_ref, down_ref, up_ref):
    for d in range(16):
        for s in range(4):
            rows = parts_ref[d, 4 * s : 4 * s + 4, :]
            down_ref[s, 4 * d : 4 * d + 4, :] = rows[:, :320]
            up_ref[s, 4 * d : 4 * d + 4, :] = rows[:, 320:]


def masked_rows(live_ref, cotangent_ref):
    count = cotangent_ref.shape[0]
    row = lax.broadcasted_iota(jnp.int32, (count, 1), 0)
    limit = jnp.where(row < BLOCK_LENGTH, live_ref[0], live_ref[1] + BLOCK_LENGTH)
    grads = cotangent_ref[...]
    return jnp.where(row < limit, grads, jnp.zeros_like(grads))


def shard_of(cell, j):
    z = cell * 2 + (8 - j if j < 4 else 1 + j - 4)
    return lax.rem(z, 8)


def block_kernel(
    cell_ref,
    tokens_ref,
    grads,
    maps_ref,
    terms_ref,
    back_out,
    wide_out,
    back_ref,
    wide_ref,
    back_sem,
    wide_sems,
):
    f32, bf16 = jnp.float32, jnp.bfloat16
    shards = [shard_of(cell_ref[0], j) for j in range(8)]
    leaving = []

    def send(source, target, sem):
        copy = pltpu.make_async_copy(source, target, sem)
        copy.start()
        leaving.append(copy)

    def token_columns(j):
        return tokens_ref[:, pl.ds(pl.multiple_of(shards[j] * 640, 128), 640)]

    def grad_columns(j):
        return grads[:, pl.ds(pl.multiple_of(shards[j] * 128, 128), 128)]

    low = lax.broadcasted_iota(jnp.int32, (128, 128), 1) < 64
    contract = (((1,), (1,)), ((), ()))
    over_rows = (((0,), (0,)), ((), ()))
    row = lax.broadcasted_iota(jnp.int32, (256, 128), 0)
    column = lax.broadcasted_iota(jnp.int32, (256, 128), 1)
    own = (row // 128) == ((column // 4) % 2)

    back = jnp.zeros((256, 128), f32)
    for j in range(8):
        k, v = j % 4, j // 4
        tiles = [
            maps_ref[2 * v + c, :, k * GROUP + 128 * i : k * GROUP + 128 * i + 128].astype(f32)
            for c in range(2)
            for i in range(3)
        ]
        turned = [None, None] + [pltpu.roll(t, 64, 1) for t in tiles[2:]]
        wide = [
            tiles[0],
            tiles[1],
            jnp.where(low, tiles[2], turned[3]),
            jnp.where(low, turned[3], turned[4]),
            jnp.where(low, turned[4], turned[5]),
        ]
        wide_ref[j] = jnp.concatenate(wide, axis=1).astype(bf16)
        send(wide_ref.at[j], wide_out.at[shards[j]], wide_sems.at[j])
        up = jnp.where(low, turned[2], tiles[5]).astype(bf16)
        back = back + lax.dot_general(grad_columns(j), up, contract, preferred_element_type=f32)
    back = jnp.where(own, adapter_scale * back, 0.0).astype(bf16)
    back_ref[...] = back
    send(back_ref, back_out, back_sem)

    down = jnp.zeros((256, 128), f32)
    for j in range(8):
        k, v = j % 4, j // 4
        rows = token_columns(j)
        part = lax.dot_general(back, rows, over_rows, preferred_element_type=f32)
        part = part * (1.0 / BLOCK_LENGTH)
        down = down + lax.dot_general(rows, wide_ref[j], contract, preferred_element_type=f32)
        piece = [part[:, 128 * i : 128 * i + 128] for i in range(5)]
        turned = [None, None] + [pltpu.roll(t, 64, 1) for t in piece[2:]]
        out = [
            piece[0],
            piece[1],
            piece[2],
            jnp.where(low, turned[2], turned[3]),
            jnp.where(low, turned[3], turned[4]),
            turned[4],
        ]
        for c in range(2):
            for i in range(3):
                at = k * GROUP + 128 * i
                terms_ref[2 * v + c, :, at : at + 128] = out[3 * c + i].astype(bf16)
    down = jnp.where(own, down, 0.0).astype(bf16)
    for j in range(8):
        k, v = j % 4, j // 4
        up = lax.dot_general(down, grad_columns(j), over_rows, preferred_element_type=f32)
        up = up * (adapter_scale / BLOCK_LENGTH)
        for c, value in enumerate((pltpu.roll(up, 64, 1), up)):
            at = slice(k * GROUP + 256, k * GROUP + 384)
            kept = terms_ref[2 * v + c, :, at]
            terms_ref[2 * v + c, :, at] = jnp.where(low, kept, value.astype(bf16))
    for copy in leaving:
        copy.wait()


def met_at(k, where_ref):
    return ((k & 1) * 7) ^ (k & 2) ^ (k >> 2) ^ where_ref[1]


def input_kernel(where_ref, masked_ref, back_ref, wide_ref, own_ref, other_ref, out_ref, weight):
    low_rank = jnp.dot(back_ref[...], wide_ref[0], preferred_element_type=jnp.float32)
    low_rank = low_rank.astype(jnp.bfloat16).astype(jnp.float32)
    core = where_ref[0]
    for start, source in ((core * 320, own_ref), (320 - core * 320, other_ref)):
        for d in range(16):
            rows = pl.ds(pl.multiple_of(start + d // 4 * 80, 80), 80)
            columns = slice(d % 4 * 256, d % 4 * 256 + 256)
            weight[rows, columns] = source[d, 0]
    frozen = lax.dot_general(
        masked_ref[...], weight[...], (((1,), (1,)), ((), ())), preferred_element_type=jnp.float32
    )
    out_ref[...] = (frozen + low_rank).astype(jnp.bfloat16)


def double(pieces, m):
    met = lax.ppermute(pieces, COLUMN, [(z, z ^ m) for z in range(8)])
    return jnp.concatenate([pieces, met], axis=0)


def on_device(
    tokens,
    cotangent,
    block_adapter,
    live_length,
    storage_row_of_adapter,
    value_weight,
    adapter_down_weight,
    adapter_up_weight,
):
    bf16, f32 = jnp.bfloat16, jnp.float32
    x, y = lax.axis_index("x"), lax.axis_index("y")
    pieces = lax.dynamic_slice(value_weight, (x * 80, y * 256), (80, 256))[None]
    pieces = double(pieces, 7)

    named = block_adapter[:, :1] == jnp.arange(64, dtype=jnp.int32)[None, :]
    near = jnp.sum(jnp.where(named, storage_row_of_adapter[None, :], 0), axis=1)
    near = jnp.pad(near, (0, 126))[None]
    swap = [(0, 1), (1, 0)]
    seen = [
        near,
        lax.ppermute(near, "c", swap),
        lax.ppermute(near, "v", swap),
        lax.ppermute(near, ("v", "c"), [(i, 3 - i) for i in range(4)]),
    ]

    smem = pl.BlockSpec(memory_space=pltpu.SMEM)
    vmem = pl.BlockSpec(memory_space=pltpu.VMEM)
    hbm = pl.BlockSpec(memory_space=pltpu.HBM)
    in_hbm = lambda x: pltpu.with_memory_space_constraint(x, pltpu.HBM)
    own = pl.pallas_call(
        pack_kernel,
        out_shape=pltpu.HBM((16, 16, GROUP + 128), bf16),
        in_specs=[hbm, hbm],
        out_specs=vmem,
        scratch_shapes=[
            pltpu.VMEM((4, 64, 320), bf16),
            pltpu.VMEM((4, 64, 64), bf16),
            pltpu.SemaphoreType.DMA((2,)),
        ],
        compiler_params=BIG,
        name="pack_maps",
    )(in_hbm(jnp.transpose(adapter_down_weight, (0, 2, 1))), in_hbm(adapter_up_weight))
    own = pl.pallas_call(
        slot_kernel,
        out_shape=pltpu.HBM((16, 16, GROUP + 128), bf16),
        in_specs=[vmem, vmem, vmem, vmem, hbm],
        out_specs=hbm,
        scratch_shapes=[pltpu.VMEM((16, 16, 128), bf16), pltpu.SemaphoreType.DMA],
        input_output_aliases={4: 0},
        compiler_params=BIG,
        name="add_slots",
    )(*seen, own)
    pieces, _ = lax.optimization_barrier((pieces, own))
    pieces = double(double(pieces, 2), 1)
    first = lax.all_to_all(own, DP, split_axis=0, concat_axis=0, tiled=True)
    table = first[:, :, :GROUP].reshape(256, GROUP)

    tables = [table] + [lax.ppermute(table, COLUMN, HEAR[k]) for k in (1, 2, 3)]

    seen = first[:, :4, GROUP : GROUP + 2].astype(jnp.int32)
    place = lax.axis_index("v") * 2 + lax.axis_index("c")
    index = jnp.arange(4, dtype=jnp.int32)
    match = (index[:, None] ^ index[None, :]) == place
    cell_slots = jnp.sum(jnp.where(match[:, None, :, None], seen[None], 0), axis=2)
    target = (cell_slots.reshape(128, 1) * 4 + jnp.arange(4, dtype=jnp.int32)[None, :]).reshape(512)

    live, _ = lax.optimization_barrier((live_length, table))
    masked = pl.pallas_call(
        mask_kernel,
        out_shape=pltpu.VMEM((256, 1024), bf16),
        in_specs=[smem, vmem],
        out_specs=vmem,
        compiler_params=BIG,
        name="mask_rows",
    )(live, cotangent)
    target_row = target.reshape(1, 512)
    cell = lax.axis_index("u").astype(jnp.int32).reshape(1)
    tables, masked, target_row, cell = lax.optimization_barrier((tables, masked, target_row, cell))
    pieces, _ = lax.optimization_barrier((pieces, table))
    half = lax.all_gather(pieces, DP, axis=0, tiled=False)

    chosen = pl.pallas_call(
        select_kernel,
        out_shape=jax.ShapeDtypeStruct((512, 4 * GROUP), bf16),
        compiler_params=BIG,
        name="select_rows",
    )(target.reshape(512, 1), *tables)
    maps = lax.all_to_all(
        chosen.reshape(64, 8, 4 * GROUP), CELL, split_axis=0, concat_axis=0, tiled=True
    ).reshape(4, 128, 4 * GROUP)

    terms, back, wide = pl.pallas_call(
        block_kernel,
        out_shape=(
            jax.ShapeDtypeStruct((4, 128, 4 * GROUP), bf16),
            pltpu.HBM((256, 128), bf16),
            pltpu.HBM((8, 128, 640), bf16),
        ),
        in_specs=[smem, vmem, vmem, vmem],
        out_specs=(vmem, hbm, hbm),
        scratch_shapes=[
            pltpu.VMEM((256, 128), bf16),
            pltpu.VMEM((8, 128, 640), bf16),
            pltpu.SemaphoreType.DMA,
            pltpu.SemaphoreType.DMA((8,)),
        ],
        compiler_params=BIG,
        cost_estimate=pl.CostEstimate(flops=10**9, bytes_accessed=9 * 10**6, transcendentals=0),
        name="block_terms",
    )(cell, tokens, masked, maps)

    returned = lax.all_to_all(
        terms.reshape(64, 8, 4 * GROUP), CELL, split_axis=0, concat_axis=0, tiled=True
    ).reshape(512, 4 * GROUP)
    sums = pl.pallas_call(
        collect_kernel,
        out_shape=(jax.ShapeDtypeStruct((256, GROUP), f32),)
        + (jax.ShapeDtypeStruct((256, GROUP), bf16),) * 3,
        compiler_params=BIG,
        name="collect_rows",
    )(target_row, returned)
    parts = [sums[0]] + [lax.ppermute(sums[k], COLUMN, TELL[k]) for k in (1, 2, 3)]
    half, _ = lax.optimization_barrier((half, sums[1]))
    other = lax.ppermute(half, "c", [(0, 1), (1, 0)])
    where = jnp.stack(
        [lax.axis_index("c"), lax.axis_index("u") * 2 + lax.axis_index("v")]
    ).astype(jnp.int32)
    weight_block = pl.BlockSpec((16, 1, 80, 256), lambda k, w: (0, k, 0, 0))
    input_grad = pl.pallas_call(
        input_kernel,
        out_shape=jax.ShapeDtypeStruct((256, 5120), bf16),
        grid_spec=pltpu.PrefetchScalarGridSpec(
            num_scalar_prefetch=1,
            grid=(8,),
            in_specs=[
                pl.BlockSpec((256, 1024), lambda k, w: (0, 0)),
                pl.BlockSpec((256, 128), lambda k, w: (0, 0)),
                pl.BlockSpec((1, 128, 640), lambda k, w: (met_at(k, w), 0, 0)),
                weight_block,
                weight_block,
            ],
            out_specs=pl.BlockSpec((256, 640), lambda k, w: (0, met_at(k, w))),
            scratch_shapes=[pltpu.VMEM((640, 1024), bf16)],
        ),
        compiler_params=BIG,
        cost_estimate=pl.CostEstimate(
            flops=3 * 10**9, bytes_accessed=16 * 10**6, transcendentals=0
        ),
        name="input_grad",
    )(where, masked, back, wide, in_hbm(half), other)
    parts[3], input_grad = lax.optimization_barrier((parts[3], input_grad))
    merged = pl.pallas_call(
        merge_kernel,
        out_shape=jax.ShapeDtypeStruct((256, GROUP), f32),
        compiler_params=BIG,
        name="merge_sums",
    )(*parts)
    parts = lax.all_to_all(
        merged.reshape(16, 16, GROUP), DP, split_axis=0, concat_axis=0, tiled=True
    )
    down, grad_up = pl.pallas_call(
        finish_kernel,
        out_shape=(
            jax.ShapeDtypeStruct((4, 64, 320), f32),
            jax.ShapeDtypeStruct((4, 64, 64), f32),
        ),
        compiler_params=BIG,
        name="finish_sums",
    )(parts)
    grad_down = jnp.transpose(down, (0, 2, 1))

    return (input_grad, grad_down, grad_up)


def solution(mesh):
    fine = Mesh(mesh.devices.reshape(4, 4, 4, 2, 2), EVERY)
    placed = (
        P(EVERY, None),
        P(EVERY, None),
        P(EVERY, None),
        P(EVERY),
        P(),
        P(FSDP, None),
        P(DP, FSDP, None),
        P(DP, None, FSDP),
    )
    return jax.shard_map(
        on_device,
        mesh=fine,
        in_specs=placed,
        out_specs=(P(EVERY, None), P(DP, FSDP, None), P(DP, None, FSDP)),
        check_vma=False,
    )
```

```python
import jax
import jax.numpy as jnp
from jax import lax
from jax.experimental import pallas as pl
from jax.experimental.pallas import tpu as pltpu
from jax.sharding import Mesh
from jax.sharding import PartitionSpec as P

BLOCK_LENGTH = 128
adapter_scale = 2.0

EVERY = ("x", "y", "u", "v", "c")
DP = ("x", "y")
COLUMN = ("u", "v")
FSDP = ("u", "v", "c")
CELL = ("v", "c", "x", "y")
HEAR = [[((z - k) % 8 if z % 2 == 0 else (z + k) % 8, z) for z in range(8)] for k in range(4)]
TELL = [[(b, a) for a, b in pairs] for pairs in HEAR]
GROUP = 384
BIG = pltpu.CompilerParams(vmem_limit_bytes=20 * 1024 * 1024)


def pack_kernel(down_hbm, up_hbm, out_ref, down_ref, up_ref, sems):
    f32, bf16 = jnp.float32, jnp.bfloat16
    copies = [
        pltpu.make_async_copy(down_hbm, down_ref, sems.at[0]),
        pltpu.make_async_copy(up_hbm, up_ref, sems.at[1]),
    ]
    for copy in copies:
        copy.start()
    for copy in copies:
        copy.wait()
    maps = [
        jnp.concatenate([down_ref[s].astype(f32), up_ref[s].astype(f32)], axis=1) for s in range(4)
    ]
    for d in range(16):
        rows = jnp.concatenate([m[4 * d : 4 * d + 4] for m in maps], axis=0)
        out_ref[d, :, :GROUP] = rows.astype(bf16)


def slot_kernel(near_ref, core_ref, level_ref, both_ref, packed_ref, out_ref, tile_ref, sem):
    line = lax.broadcasted_iota(jnp.int32, (16, 128), 0)
    slots = jnp.zeros((16, 128), jnp.int32)
    for i, ref in enumerate((near_ref, core_ref, level_ref, both_ref)):
        slots = jnp.where(line == i, jnp.broadcast_to(ref[...], (16, 128)), slots)
    slots = slots.astype(jnp.float32).astype(jnp.bfloat16)
    for d in range(16):
        tile_ref[d] = slots
    copy = pltpu.make_async_copy(tile_ref, out_ref.at[:, :, GROUP:], sem)
    copy.start()
    copy.wait()


def mask_kernel(live_ref, cotangent_ref, grads_ref):
    grads_ref[...] = masked_rows(live_ref, cotangent_ref)


def select_kernel(target_ref, table0, table1, table2, table3, out_ref):
    rows = out_ref.shape[0]
    lane = lax.broadcasted_iota(jnp.int32, (rows, 256), 1)
    pick = jnp.where(lane == target_ref[...], 1.0, 0.0).astype(jnp.bfloat16)
    for k, table in enumerate((table0, table1, table2, table3)):
        part = jnp.dot(pick, table[...], preferred_element_type=jnp.float32)
        out_ref[:, k * GROUP : (k + 1) * GROUP] = part.astype(jnp.bfloat16)


def collect_kernel(target_ref, terms_ref, out0, out1, out2, out3):
    rows = terms_ref.shape[0]
    sub = lax.broadcasted_iota(jnp.int32, (256, rows), 0)
    pick = jnp.where(sub == target_ref[...], 1.0, 0.0).astype(jnp.bfloat16)
    for k, out in enumerate((out0, out1, out2, out3)):
        part = jnp.dot(
            pick, terms_ref[:, k * GROUP : (k + 1) * GROUP], preferred_element_type=jnp.float32
        )
        out[...] = part.astype(out.dtype)


def merge_kernel(part0, part1, part2, part3, out_ref):
    f32 = jnp.float32
    total = (part0[...] + part1[...].astype(f32)) + (
        part2[...].astype(f32) + part3[...].astype(f32)
    )
    out_ref[...] = total.astype(out_ref.dtype)


def finish_kernel(parts_ref, down_ref, up_ref):
    for d in range(16):
        group = parts_ref[d].astype(jnp.float32)
        for s in range(4):
            rows = group[4 * s : 4 * s + 4]
            down_ref[s, 4 * d : 4 * d + 4, :] = rows[:, :320]
            up_ref[s, 4 * d : 4 * d + 4, :] = rows[:, 320:]


def masked_rows(live_ref, cotangent_ref):
    count = cotangent_ref.shape[0]
    row = lax.broadcasted_iota(jnp.int32, (count, 1), 0)
    limit = jnp.where(row < BLOCK_LENGTH, live_ref[0], live_ref[1] + BLOCK_LENGTH)
    grads = cotangent_ref[...]
    return jnp.where(row < limit, grads, jnp.zeros_like(grads))


def shard_of(cell, j):
    z = cell * 2 + (8 - j if j < 4 else 1 + j - 4)
    return lax.rem(z, 8)


def block_kernel(
    cell_ref,
    tokens_ref,
    grads,
    maps_ref,
    terms_ref,
    back_out,
    wide_out,
    back_ref,
    wide_ref,
    back_sem,
    wide_sems,
):
    f32, bf16 = jnp.float32, jnp.bfloat16
    shards = [shard_of(cell_ref[0], j) for j in range(8)]
    leaving = []

    def send(source, target, sem):
        copy = pltpu.make_async_copy(source, target, sem)
        copy.start()
        leaving.append(copy)

    def token_columns(j):
        return tokens_ref[:, pl.ds(pl.multiple_of(shards[j] * 640, 128), 640)]

    def grad_columns(j):
        return grads[:, pl.ds(pl.multiple_of(shards[j] * 128, 128), 128)]

    low = lax.broadcasted_iota(jnp.int32, (128, 128), 1) < 64
    contract = (((1,), (1,)), ((), ()))
    over_rows = (((0,), (0,)), ((), ()))
    row = lax.broadcasted_iota(jnp.int32, (256, 128), 0)
    column = lax.broadcasted_iota(jnp.int32, (256, 128), 1)
    own = (row // 128) == ((column // 4) % 2)

    back = jnp.zeros((256, 128), f32)
    for j in range(8):
        k, v = j % 4, j // 4
        tiles = [
            maps_ref[2 * v + c, :, k * GROUP + 128 * i : k * GROUP + 128 * i + 128].astype(f32)
            for c in range(2)
            for i in range(3)
        ]
        turned = [None, None] + [pltpu.roll(t, 64, 1) for t in tiles[2:]]
        wide = [
            tiles[0],
            tiles[1],
            jnp.where(low, tiles[2], turned[3]),
            jnp.where(low, turned[3], turned[4]),
            jnp.where(low, turned[4], turned[5]),
        ]
        wide_ref[j] = jnp.concatenate(wide, axis=1).astype(bf16)
        send(wide_ref.at[j], wide_out.at[shards[j]], wide_sems.at[j])
        up = jnp.where(low, turned[2], tiles[5]).astype(bf16)
        back = back + lax.dot_general(grad_columns(j), up, contract, preferred_element_type=f32)
    back = jnp.where(own, adapter_scale * back, 0.0).astype(bf16)
    back_ref[...] = back
    send(back_ref, back_out, back_sem)

    down = jnp.zeros((256, 128), f32)
    for j in range(8):
        k, v = j % 4, j // 4
        rows = token_columns(j)
        part = lax.dot_general(back, rows, over_rows, preferred_element_type=f32)
        part = part * (1.0 / BLOCK_LENGTH)
        down = down + lax.dot_general(rows, wide_ref[j], contract, preferred_element_type=f32)
        piece = [part[:, 128 * i : 128 * i + 128] for i in range(5)]
        turned = [None, None] + [pltpu.roll(t, 64, 1) for t in piece[2:]]
        out = [
            piece[0],
            piece[1],
            piece[2],
            jnp.where(low, turned[2], turned[3]),
            jnp.where(low, turned[3], turned[4]),
            turned[4],
        ]
        for c in range(2):
            for i in range(3):
                at = k * GROUP + 128 * i
                terms_ref[2 * v + c, :, at : at + 128] = out[3 * c + i].astype(bf16)
    down = jnp.where(own, down, 0.0).astype(bf16)
    for j in range(8):
        k, v = j % 4, j // 4
        up = lax.dot_general(down, grad_columns(j), over_rows, preferred_element_type=f32)
        up = up * (adapter_scale / BLOCK_LENGTH)
        for c, value in enumerate((pltpu.roll(up, 64, 1), up)):
            at = slice(k * GROUP + 256, k * GROUP + 384)
            kept = terms_ref[2 * v + c, :, at]
            terms_ref[2 * v + c, :, at] = jnp.where(low, kept, value.astype(bf16))
    for copy in leaving:
        copy.wait()


def met_at(k, where_ref):
    return ((k & 1) * 7) ^ (k & 2) ^ (k >> 2) ^ where_ref[1]


def input_kernel(where_ref, masked_ref, back_ref, wide_ref, own_ref, other_ref, out_ref, weight):
    low_rank = jnp.dot(back_ref[...], wide_ref[0], preferred_element_type=jnp.float32)
    low_rank = low_rank.astype(jnp.bfloat16).astype(jnp.float32)
    core = where_ref[0]
    for start, source in ((core * 320, own_ref), (320 - core * 320, other_ref)):
        for d in range(16):
            rows = pl.ds(pl.multiple_of(start + d // 4 * 80, 80), 80)
            columns = slice(d % 4 * 256, d % 4 * 256 + 256)
            weight[rows, columns] = source[d, 0]
    frozen = lax.dot_general(
        masked_ref[...], weight[...], (((1,), (1,)), ((), ())), preferred_element_type=jnp.float32
    )
    out_ref[...] = (frozen + low_rank).astype(jnp.bfloat16)


def double(pieces, m):
    met = lax.ppermute(pieces, COLUMN, [(z, z ^ m) for z in range(8)])
    return jnp.concatenate([pieces, met], axis=0)


def on_device(
    tokens,
    cotangent,
    block_adapter,
    live_length,
    storage_row_of_adapter,
    value_weight,
    adapter_down_weight,
    adapter_up_weight,
):
    bf16, f32 = jnp.bfloat16, jnp.float32
    x, y = lax.axis_index("x"), lax.axis_index("y")
    pieces = lax.dynamic_slice(value_weight, (x * 80, y * 256), (80, 256))[None]
    pieces = double(pieces, 7)

    named = block_adapter[:, :1] == jnp.arange(64, dtype=jnp.int32)[None, :]
    near = jnp.sum(jnp.where(named, storage_row_of_adapter[None, :], 0), axis=1)
    near = jnp.pad(near, (0, 126))[None]
    swap = [(0, 1), (1, 0)]
    seen = [
        near,
        lax.ppermute(near, "c", swap),
        lax.ppermute(near, "v", swap),
        lax.ppermute(near, ("v", "c"), [(i, 3 - i) for i in range(4)]),
    ]

    smem = pl.BlockSpec(memory_space=pltpu.SMEM)
    vmem = pl.BlockSpec(memory_space=pltpu.VMEM)
    hbm = pl.BlockSpec(memory_space=pltpu.HBM)
    in_hbm = lambda x: pltpu.with_memory_space_constraint(x, pltpu.HBM)
    own = pl.pallas_call(
        pack_kernel,
        out_shape=pltpu.HBM((16, 16, GROUP + 128), bf16),
        in_specs=[hbm, hbm],
        out_specs=vmem,
        scratch_shapes=[
            pltpu.VMEM((4, 64, 320), bf16),
            pltpu.VMEM((4, 64, 64), bf16),
            pltpu.SemaphoreType.DMA((2,)),
        ],
        compiler_params=BIG,
        name="pack_maps",
    )(in_hbm(jnp.transpose(adapter_down_weight, (0, 2, 1))), in_hbm(adapter_up_weight))
    own = pl.pallas_call(
        slot_kernel,
        out_shape=pltpu.HBM((16, 16, GROUP + 128), bf16),
        in_specs=[vmem, vmem, vmem, vmem, hbm],
        out_specs=hbm,
        scratch_shapes=[pltpu.VMEM((16, 16, 128), bf16), pltpu.SemaphoreType.DMA],
        input_output_aliases={4: 0},
        compiler_params=BIG,
        name="add_slots",
    )(*seen, own)
    pieces, _ = lax.optimization_barrier((pieces, own))
    pieces = double(double(pieces, 2), 1)
    first = lax.all_to_all(own, DP, split_axis=0, concat_axis=0, tiled=True)
    table = first[:, :, :GROUP].reshape(256, GROUP)

    tables = [table] + [lax.ppermute(table, COLUMN, HEAR[k]) for k in (1, 2, 3)]

    seen = first[:, :4, GROUP : GROUP + 2].astype(jnp.int32)
    place = lax.axis_index("v") * 2 + lax.axis_index("c")
    index = jnp.arange(4, dtype=jnp.int32)
    match = (index[:, None] ^ index[None, :]) == place
    cell_slots = jnp.sum(jnp.where(match[:, None, :, None], seen[None], 0), axis=2)
    target = (cell_slots.reshape(128, 1) * 4 + jnp.arange(4, dtype=jnp.int32)[None, :]).reshape(512)

    live, _ = lax.optimization_barrier((live_length, table))
    masked = pl.pallas_call(
        mask_kernel,
        out_shape=pltpu.VMEM((256, 1024), bf16),
        in_specs=[smem, vmem],
        out_specs=vmem,
        compiler_params=BIG,
        name="mask_rows",
    )(live, cotangent)
    target_row = target.reshape(1, 512)
    cell = lax.axis_index("u").astype(jnp.int32).reshape(1)
    tables, masked, target_row, cell = lax.optimization_barrier((tables, masked, target_row, cell))
    pieces, _ = lax.optimization_barrier((pieces, table))
    half = lax.all_gather(pieces, DP, axis=0, tiled=False)

    chosen = pl.pallas_call(
        select_kernel,
        out_shape=jax.ShapeDtypeStruct((512, 4 * GROUP), bf16),
        compiler_params=BIG,
        name="select_rows",
    )(target.reshape(512, 1), *tables)
    maps = lax.all_to_all(
        chosen.reshape(64, 8, 4 * GROUP), CELL, split_axis=0, concat_axis=0, tiled=True
    ).reshape(4, 128, 4 * GROUP)

    terms, back, wide = pl.pallas_call(
        block_kernel,
        out_shape=(
            jax.ShapeDtypeStruct((4, 128, 4 * GROUP), bf16),
            pltpu.HBM((256, 128), bf16),
            pltpu.HBM((8, 128, 640), bf16),
        ),
        in_specs=[smem, vmem, vmem, vmem],
        out_specs=(vmem, hbm, hbm),
        scratch_shapes=[
            pltpu.VMEM((256, 128), bf16),
            pltpu.VMEM((8, 128, 640), bf16),
            pltpu.SemaphoreType.DMA,
            pltpu.SemaphoreType.DMA((8,)),
        ],
        compiler_params=BIG,
        cost_estimate=pl.CostEstimate(flops=10**9, bytes_accessed=9 * 10**6, transcendentals=0),
        name="block_terms",
    )(cell, tokens, masked, maps)

    returned = lax.all_to_all(
        terms.reshape(64, 8, 4 * GROUP), CELL, split_axis=0, concat_axis=0, tiled=True
    ).reshape(512, 4 * GROUP)
    sums = pl.pallas_call(
        collect_kernel,
        out_shape=(jax.ShapeDtypeStruct((256, GROUP), f32),)
        + (jax.ShapeDtypeStruct((256, GROUP), bf16),) * 3,
        compiler_params=BIG,
        name="collect_rows",
    )(target_row, returned)
    parts = [sums[0]] + [lax.ppermute(sums[k], COLUMN, TELL[k]) for k in (1, 2, 3)]
    half, _ = lax.optimization_barrier((half, sums[1]))
    other = lax.ppermute(half, "c", [(0, 1), (1, 0)])
    where = jnp.stack(
        [lax.axis_index("c"), lax.axis_index("u") * 2 + lax.axis_index("v")]
    ).astype(jnp.int32)
    weight_block = pl.BlockSpec((16, 1, 80, 256), lambda k, w: (0, k, 0, 0))
    input_grad = pl.pallas_call(
        input_kernel,
        out_shape=jax.ShapeDtypeStruct((256, 5120), bf16),
        grid_spec=pltpu.PrefetchScalarGridSpec(
            num_scalar_prefetch=1,
            grid=(8,),
            in_specs=[
                pl.BlockSpec((256, 1024), lambda k, w: (0, 0)),
                pl.BlockSpec((256, 128), lambda k, w: (0, 0)),
                pl.BlockSpec((1, 128, 640), lambda k, w: (met_at(k, w), 0, 0)),
                weight_block,
                weight_block,
            ],
            out_specs=pl.BlockSpec((256, 640), lambda k, w: (0, met_at(k, w))),
            scratch_shapes=[pltpu.VMEM((640, 1024), bf16)],
        ),
        compiler_params=BIG,
        cost_estimate=pl.CostEstimate(
            flops=3 * 10**9, bytes_accessed=16 * 10**6, transcendentals=0
        ),
        name="input_grad",
    )(where, masked, back, wide, in_hbm(half), other)
    parts[3], input_grad = lax.optimization_barrier((parts[3], input_grad))
    merged = pl.pallas_call(
        merge_kernel,
        out_shape=jax.ShapeDtypeStruct((256, GROUP), bf16),
        compiler_params=BIG,
        name="merge_sums",
    )(*parts)
    parts = lax.all_to_all(
        merged.reshape(16, 16, GROUP), DP, split_axis=0, concat_axis=0, tiled=True
    )
    down, grad_up = pl.pallas_call(
        finish_kernel,
        out_shape=(
            jax.ShapeDtypeStruct((4, 64, 320), f32),
            jax.ShapeDtypeStruct((4, 64, 64), f32),
        ),
        compiler_params=BIG,
        name="finish_sums",
    )(parts)
    grad_down = jnp.transpose(down, (0, 2, 1))

    return (input_grad, grad_down, grad_up)


def solution(mesh):
    fine = Mesh(mesh.devices.reshape(4, 4, 4, 2, 2), EVERY)
    placed = (
        P(EVERY, None),
        P(EVERY, None),
        P(EVERY, None),
        P(EVERY),
        P(),
        P(FSDP, None),
        P(DP, FSDP, None),
        P(DP, None, FSDP),
    )
    return jax.shard_map(
        on_device,
        mesh=fine,
        in_specs=placed,
        out_specs=(P(EVERY, None), P(DP, FSDP, None), P(DP, None, FSDP)),
        check_vma=False,
    )
```
